256 devices in a mesh: seq: 16 (over z, core), head: 16 (over x, y).
Axes of the slice: x: 4, y: 4, z: 8, core: 2. Of those that a mesh axis runs over, the one named last changes fastest.
Arguments:
- features: bfloat16 [65536, 8192], P(('seq', 'head')), may hold values from -6 to 6
- step_size: float32 [65536, 128], P(('seq', 'head')), may hold values from 0.01 to 0.08
- log_decay: float32 [65536, 128], P(('seq', 'head')), may hold values from -0.6 to 0
- inject: bfloat16 [65536, 1024], P(('seq', 'head')), may hold values from -1.5 to 1.5
- readout: bfloat16 [65536, 1024], P(('seq', 'head')), may hold values from -1.5 to 1.5
- skip_gain: float32 [128], replicated, may hold values from 0.5 to 1.5
Outputs:
- mixer_out: bfloat16 [65536, 8192], P(('seq', 'head'))
The draws below stay inside these ranges and needn't reach their ends.
All inputs are finite; a program needn't handle non-finite values.
Results may differ from the reference program's by a relative error of at most 0.02.
Values may be sent and summed in bfloat16 or wider, within the bound.
No kernel may reach another device: no remote copies, remote signals or barrier semaphores. Data moves between devices by JAX's collectives and lax.ppermute only.
A program may use at most 128 MiB of HBM per device.

```python
import math
import jax
import jax.numpy as jnp
from jax import lax

MIXER_HEADS = 128
HEAD_DIM = 64
STATE = 128
GROUPS = 8
SPAN = 512
TOK_DEV = 256
TOKENS = 65536


def draw_log_decay(key, part):
    random_subkeys = jax.random.split(key, 7)
    fast_share = 0.5
    fast_heads = jax.random.uniform(random_subkeys[0], (MIXER_HEADS,), jnp.float32) < fast_share
    fast_rate = jnp.exp(jax.random.uniform(random_subkeys[1], (MIXER_HEADS,), jnp.float32, math.log(1.0 / 50.0), math.log(1.0 / 25.0)))
    slow_rate = jnp.exp(jax.random.uniform(random_subkeys[2], (MIXER_HEADS,), jnp.float32, math.log(0.3), math.log(0.6))) / TOKENS
    head_rate = jnp.where(fast_heads, fast_rate, slow_rate)
    block_count = TOKENS // TOK_DEV
    factor = jnp.exp(jax.random.uniform(random_subkeys[3], (block_count, 1), jnp.float32, math.log(0.5), math.log(2.0)))
    factor = jnp.repeat(factor, TOK_DEV, axis=0)
    roughness = jax.random.uniform(random_subkeys[4], (TOKENS, MIXER_HEADS), jnp.float32, 0.5, 1.5)
    baseline_portion = -head_rate[None, :] * factor * roughness
    token_positions = jax.random.randint(random_subkeys[5], (3,), 0, TOKENS)
    surge_length = jax.random.uniform(random_subkeys[6], (3, MIXER_HEADS), jnp.float32, 0.22, 0.45)
    token_identifiers = jnp.arange(TOKENS, dtype=jnp.int32)
    surge_selected = (token_identifiers[:, None] == token_positions[None, :]).astype(jnp.float32)
    surge_portion = jnp.sum(surge_selected[:, :, None] * surge_length[None, :, :], axis=1)
    return (baseline_portion - surge_portion).astype(jnp.float32)


def levels(key, extent, cuts, low, high):
    loudness, own = 1.0, jax.random.fold_in(key, 6)
    for axis_at, shards_of in cuts:
        draws = jnp.exp(jax.random.uniform(jax.random.fold_in(own, axis_at), (shards_of,), jnp.float32, low / len(cuts), high / len(cuts)))
        loudness = loudness * jnp.repeat(draws, extent[axis_at] // shards_of).reshape([-1 if axis == axis_at else 1 for axis in range(len(extent))])
    return loudness


def bell_draw(key, extent, deviation, most, shards=(), kind=jnp.bfloat16):
    loudness = levels(key, extent, shards, -0.22, 0.18) if shards else 1.0
    values = jax.random.normal(key, extent, jnp.float32) * deviation * loudness
    return jnp.minimum(jnp.maximum(values, -most), most).astype(kind)


def setup_inputs(seed: int = 0) -> dict:
    key_of = jax.random.split(jax.random.key(seed), 7)
    features = bell_draw(key_of[0], (TOKENS, MIXER_HEADS * HEAD_DIM), 1.0, 6.0, ((0, 256),))
    step_size = jnp.clip(jnp.exp(math.log(0.08) - 2.0794415 * jax.random.uniform(key_of[1], (TOKENS, MIXER_HEADS), jnp.float32) ** levels(key_of[1], (TOKENS, MIXER_HEADS), ((0, 256),), -0.2, 0.2)), 0.01, 0.08)
    log_decay = draw_log_decay(jax.random.fold_in(key_of[6], 71), 0)
    inject = bell_draw(key_of[3], (TOKENS, GROUPS * STATE), 0.25, 1.5, ((0, 256),))
    readout = bell_draw(key_of[4], (TOKENS, GROUPS * STATE), 0.25, 1.5, ((0, 256),))
    skip_gain = jnp.clip(jax.random.uniform(key_of[5], (MIXER_HEADS,), jnp.float32, 0.5, 1.5), 0.5, 1.5)
    return {"features": features, "step_size": step_size, "log_decay": log_decay, "inject": inject, "readout": readout, "skip_gain": skip_gain}


def reference(features, step_size, log_decay, inject, readout, skip_gain):
    length = features.shape[0]
    spans = length // SPAN
    per_group = MIXER_HEADS // GROUPS
    drive = (features.reshape(length, MIXER_HEADS, HEAD_DIM).astype(jnp.float32) * step_size[:, :, None]).astype(jnp.bfloat16)
    cum_all = jnp.cumsum(log_decay.reshape(spans, SPAN, MIXER_HEADS), axis=1)
    inject_q = inject.reshape(spans, SPAN, GROUPS, STATE)
    readout_q = readout.reshape(spans, SPAN, GROUPS, STATE)
    drive_q = drive.reshape(spans, SPAN, GROUPS, per_group, HEAD_DIM)
    plain_q = features.reshape(spans, SPAN, GROUPS, per_group, HEAD_DIM)
    row_ids = lax.broadcasted_iota(jnp.int32, (SPAN, SPAN), 0)
    col_ids = lax.broadcasted_iota(jnp.int32, (SPAN, SPAN), 1)
    lower_mask = row_ids >= col_ids
    gains = skip_gain.reshape(GROUPS, per_group)

    def advance(carried, pieces):
        read_c, inject_c, drive_c, cum_c, plain_c = pieces
        read_f = read_c.astype(jnp.float32)
        inject_f = inject_c.astype(jnp.float32)
        drive_f = drive_c.astype(jnp.float32)
        intersection = jnp.einsum("ign,jgn->gij", read_f, inject_f)
        cum_heads = cum_c.T
        log_gap = cum_heads[:, :, None] - cum_heads[:, None, :]
        decays = jnp.where(lower_mask, jnp.exp(jnp.where(lower_mask, log_gap, 0.0)), 0.0)
        weights = (decays.reshape(GROUPS, per_group, SPAN, SPAN) * intersection[:, None]).astype(jnp.bfloat16)
        inner_out = jnp.einsum("ghij,jghp->ighp", weights.astype(jnp.float32), drive_f)
        held = carried.astype(jnp.bfloat16).astype(jnp.float32).reshape(GROUPS, per_group, HEAD_DIM, STATE)
        outer_out = jnp.einsum("ign,ghpn->ighp", read_f, held) * jnp.exp(cum_c).reshape(SPAN, GROUPS, per_group)[..., None]
        tail_decay = jnp.exp(cum_heads[:, -1:] - cum_heads)
        scaled = (drive_f * tail_decay.T.reshape(SPAN, GROUPS, per_group)[..., None]).astype(jnp.bfloat16)
        summary = jnp.einsum("jghp,jgn->ghpn", scaled.astype(jnp.float32), inject_f).reshape(MIXER_HEADS, HEAD_DIM, STATE)
        updated = carried * jnp.exp(cum_heads[:, -1])[:, None, None] + summary
        total_out = inner_out + outer_out + gains[None, :, :, None] * plain_c.astype(jnp.float32)
        return updated, total_out.astype(jnp.bfloat16).reshape(SPAN, MIXER_HEADS * HEAD_DIM)

    start_state = jnp.zeros((MIXER_HEADS, HEAD_DIM, STATE), jnp.float32)
    final_state, outputs = lax.scan(advance, start_state, (readout_q, inject_q, drive_q, cum_all, plain_q))
    return outputs.reshape(length, MIXER_HEADS * HEAD_DIM)
```

```python
import functools

import jax
import jax.numpy as jnp
from jax import lax
from jax.experimental import pallas as pl
from jax.experimental.pallas import tpu as pltpu
from jax.sharding import PartitionSpec as P

HEADS = 128
HEAD_DIM = 64
STATE = 128
GROUPS = 8
TOK = 256
HALF = 128
LANES = 128
OWNERS = 64
STEP = 4
OWN_HEADS = HEADS // OWNERS
COLS = OWN_HEADS * HEAD_DIM
GROUP_COLS = HEADS // GROUPS * HEAD_DIM
GROUP_OWNERS = OWNERS // GROUPS
ROWS = STATE + 8
VMEM_LIMIT = 61 * 1024 * 1024
OUT_VMEM_LIMIT = 50 * 1024 * 1024
HELD_VMEM_LIMIT = 40 * 1024 * 1024
SMALL_VMEM_LIMIT = 24 * 1024 * 1024
WIDE = 512
LOCAL_PARTS = 2
PART_GROUPS = GROUPS // LOCAL_PARTS
PART_COLS = PART_GROUPS * GROUP_COLS

f32 = jnp.float32
bf16 = jnp.bfloat16


def dot(a, b):
    return jnp.dot(a, b, preferred_element_type=f32)


def dot_exact(a, b):
    return jnp.dot(a, b, preferred_element_type=f32, precision=lax.Precision.HIGHEST)


def iota(shape, axis):
    return lax.broadcasted_iota(jnp.int32, shape, axis)


def spread(scale, first_col, cols):
    place = iota((scale.shape[0], LANES), 1) >> 6
    first_head = first_col // HEAD_DIM
    return jnp.concatenate(
        [
            jnp.take_along_axis(
                scale, place + (first_head + 2 * k), axis=1, mode="promise_in_bounds"
            )
            for k in range(cols // LANES)
        ],
        axis=1,
    )


def copies(*triples):
    made = [pltpu.make_async_copy(*t) for t in triples]
    for c in made:
        c.start()
    return made


def state_kernel(
    x_hbm, step_hbm, decay_hbm, inject_hbm, out_hbm,
    x_buf, step_buf, decay_buf, inject_buf, out_buf, sem, in_sem, out_sem,
):
    decay_in, step_in, inject_in = copies(
        (decay_hbm, decay_buf, sem.at[0]),
        (step_hbm, step_buf, sem.at[1]),
        (inject_hbm, inject_buf, sem.at[2]),
    )
    x_in = copies(
        *[
            (x_hbm.at[:, pl.ds(g * GROUP_COLS, GROUP_COLS)], x_buf.at[g], in_sem.at[g])
            for g in range(GROUPS)
        ]
    )
    later = jnp.where(iota((TOK, TOK), 1) > iota((TOK, TOK), 0), 1.0, 0.0).astype(f32)
    decay_in.wait()
    decay = decay_buf[...]
    tail = dot_exact(later, decay)
    whole = jnp.broadcast_to(jnp.exp(tail[0:1] + decay[0:1]), (8, HEADS))
    high = whole.astype(bf16).astype(f32)
    row = iota((8, HEADS), 0)
    extra = jnp.where(row == 0, high, jnp.where(row == 1, whole - high, 0.0))
    step_in.wait()
    scale = step_buf[...] * jnp.exp(tail)
    inject_in.wait()
    sent = []
    for g in range(GROUPS):
        at = g * GROUP_COLS
        weight = spread(scale, at, GROUP_COLS)
        below = spread(extra, at, GROUP_COLS).astype(bf16)
        x_in[g].wait()
        v = (x_buf[g].astype(f32) * weight).astype(bf16)
        s = lax.dot_general(
            inject_buf[:, g * STATE : (g + 1) * STATE],
            v,
            (((0,), (0,)), ((), ())),
            preferred_element_type=f32,
        ).astype(bf16)
        first = g * GROUP_OWNERS
        for k in range(GROUP_OWNERS):
            cols = slice(k * COLS, (k + 1) * COLS)
            out_buf[first + k, :STATE, :] = s[:, cols]
            out_buf[first + k, STATE:, :] = below[:, cols]
        span = pl.ds(first, GROUP_OWNERS)
        sent += copies((out_buf.at[span], out_hbm.at[span], out_sem.at[g]))
    for c in sent:
        c.wait()


def states_of(x, step, decay, inject):
    hbm = pl.BlockSpec(memory_space=pltpu.HBM)
    return pl.pallas_call(
        state_kernel,
        out_shape=jax.ShapeDtypeStruct((OWNERS, ROWS, COLS), bf16),
        in_specs=[hbm] * 4,
        out_specs=hbm,
        scratch_shapes=[
            pltpu.VMEM((GROUPS, TOK, GROUP_COLS), bf16),
            pltpu.VMEM((TOK, HEADS), f32),
            pltpu.VMEM((TOK, HEADS), f32),
            pltpu.VMEM((TOK, GROUPS * STATE), bf16),
            pltpu.VMEM((OWNERS, ROWS, COLS), bf16),
            pltpu.SemaphoreType.DMA((3,)),
            pltpu.SemaphoreType.DMA((GROUPS,)),
            pltpu.SemaphoreType.DMA((GROUPS,)),
        ],
        compiler_params=pltpu.CompilerParams(vmem_limit_bytes=VMEM_LIMIT),
        cost_estimate=pl.CostEstimate(
            flops=2_000_000_000, bytes_accessed=8_000_000, transcendentals=32768
        ),
        name="states",
    )(x, step, decay, inject)


def decay_row(block):
    return block[STATE : STATE + 1].astype(f32) + block[STATE + 1 : STATE + 2].astype(f32)


def pack_rows(decay):
    row = iota((8, COLS), 0)
    high = decay.astype(bf16).astype(f32)
    return jnp.where(row == 0, high, jnp.where(row == 1, decay - high, 0.0)).astype(bf16)


def total_kernel(in_ref, out_ref):
    state = in_ref[0, :STATE, :].astype(f32)
    decay = decay_row(in_ref[0])
    for i in range(1, OWNERS):
        d = decay_row(in_ref[i])
        state = state * d + in_ref[i, :STATE, :].astype(f32)
        decay = decay * d
    out_ref[:STATE, :] = state.astype(bf16)
    out_ref[STATE:, :] = pack_rows(decay)


def held_kernel(one_ref, two_ref, three_ref, in_ref, out_hbm, out_buf, sem):
    state = three_ref[:STATE, :].astype(f32)
    for ref in (two_ref, one_ref):
        state = ref[:STATE, :].astype(f32) + decay_row(ref[...]) * state
    sent = []
    for i in range(OWNERS):
        out_buf[i] = state.astype(bf16)
        if (i + 1) % GROUPS == 0:
            span = pl.ds(i + 1 - GROUPS, GROUPS)
            sent += copies((out_buf.at[span], out_hbm.at[span], sem.at[i // GROUPS]))
        if i + 1 < OWNERS:
            state = state * decay_row(in_ref[i]) + in_ref[i, :STATE, :].astype(f32)
    for c in sent:
        c.wait()


def total_of(arrived):
    return pl.pallas_call(
        total_kernel,
        out_shape=jax.ShapeDtypeStruct((ROWS, COLS), bf16),
        compiler_params=pltpu.CompilerParams(vmem_limit_bytes=SMALL_VMEM_LIMIT),
        cost_estimate=pl.CostEstimate(flops=4_000_000, bytes_accessed=2_000_000, transcendentals=0),
        name="total",
    )(arrived)


def held_of(earlier, arrived):
    vmem = pl.BlockSpec(memory_space=pltpu.VMEM)
    return pl.pallas_call(
        held_kernel,
        out_shape=jax.ShapeDtypeStruct((OWNERS, STATE, COLS), bf16),
        in_specs=[vmem] * 4,
        out_specs=pl.BlockSpec(memory_space=pltpu.HBM),
        scratch_shapes=[
            pltpu.VMEM((OWNERS, STATE, COLS), bf16),
            pltpu.SemaphoreType.DMA((OWNERS // GROUPS,)),
        ],
        compiler_params=pltpu.CompilerParams(vmem_limit_bytes=HELD_VMEM_LIMIT),
        cost_estimate=pl.CostEstimate(flops=4_000_000, bytes_accessed=4_000_000, transcendentals=0),
        name="held",
    )(*earlier, arrived)


def local_kernel(
    part, x_hbm, step_hbm, decay_hbm, inject_hbm, readout_hbm, gain_ref, *rest
):
    (
        out_hbm, x_buf, step_buf, decay_buf, inject_buf, readout_buf, out_buf,
        sem, in_sem, out_sem,
    ) = rest[-10:]
    decay_in, step_in, inject_in, readout_in = copies(
        (decay_hbm, decay_buf, sem.at[0]),
        (step_hbm, step_buf, sem.at[1]),
        (inject_hbm, inject_buf, sem.at[2]),
        (readout_hbm, readout_buf, sem.at[3]),
    )
    x_in = copies(
        *[
            (
                x_hbm.at[:, pl.ds(part * PART_COLS + n * GROUP_COLS, GROUP_COLS)],
                x_buf.at[n],
                in_sem.at[n],
            )
            for n in range(PART_GROUPS)
        ]
    )
    lower = iota((HALF, HALF), 0) >= iota((HALF, HALF), 1)
    lower_f = jnp.where(lower, 1.0, 0.0).astype(f32)
    decay_in.wait()
    cum_a = dot_exact(lower_f, decay_buf[:HALF])
    cum_b = dot_exact(lower_f, decay_buf[HALF:])
    mid = HALF // 2 - 1
    mid_b = cum_b[mid : mid + 1]
    gap_a = cum_a - cum_a[mid : mid + 1]
    gap_b = cum_b - mid_b
    onward = jnp.exp(mid_b + gap_a[HALF - 1 : HALF])
    few = iota((8, HEADS), 0)
    rows = jnp.where(few == 0, onward, gain_ref[...])
    step_in.wait()
    into_a = step_buf[:HALF] * jnp.exp(-gap_a)
    into_b = step_buf[HALF:] * jnp.exp(-gap_b)
    from_a = jnp.exp(gap_a)
    from_b = jnp.exp(gap_b)
    zero = jnp.zeros((HALF, HALF), f32)
    inject_in.wait()
    readout_in.wait()

    def pair(r, i):
        return lax.dot_general(r, i, (((1,), (1,)), ((), ())), preferred_element_type=f32)

    sent = []
    for n in range(PART_GROUPS):
        g = part * PART_GROUPS + n
        state_cols = slice(g * STATE, (g + 1) * STATE)
        inj_a = inject_buf[:HALF, state_cols]
        inj_b = inject_buf[HALF:, state_cols]
        read_a = readout_buf[:HALF, state_cols]
        read_b = readout_buf[HALF:, state_cols]
        near_a = jnp.where(lower, pair(read_a, inj_a), zero).astype(bf16)
        near_b = jnp.concatenate(
            [
                pair(read_b, inj_a).astype(bf16),
                jnp.where(lower, pair(read_b, inj_b), zero).astype(bf16),
            ],
            axis=1,
        )
        x_in[n].wait()
        for k in range(GROUP_COLS // WIDE):
            cols = slice(k * WIDE, (k + 1) * WIDE)
            at = g * GROUP_COLS + k * WIDE
            row = spread(rows, at, WIDE)
            gain = row[1:2]
            x_a = x_buf[n, :HALF, cols].astype(f32)
            x_b = x_buf[n, HALF:, cols].astype(f32)
            v_a = x_a * spread(into_a, at, WIDE)
            v_b = (x_b * spread(into_b, at, WIDE)).astype(bf16)
            res_a = dot(near_a, v_a.astype(bf16))
            res_b = dot(near_b, jnp.concatenate([(v_a * row[0:1]).astype(bf16), v_b], axis=0))
            out_a = res_a * spread(from_a, at, WIDE) + gain * x_a
            out_b = res_b * spread(from_b, at, WIDE) + gain * x_b
            out_buf[n, :HALF, cols] = out_a.astype(bf16)
            out_buf[n, HALF:, cols] = out_b.astype(bf16)
        sent += copies(
            (out_buf.at[n], out_hbm.at[:, pl.ds(g * GROUP_COLS, GROUP_COLS)], out_sem.at[n])
        )
    for c in sent:
        c.wait()


def local_of(part, so_far, x, step, decay, inject, readout, gain):
    hbm = pl.BlockSpec(memory_space=pltpu.HBM)
    vmem = pl.BlockSpec(memory_space=pltpu.VMEM)
    return pl.pallas_call(
        functools.partial(local_kernel, part),
        out_shape=jax.ShapeDtypeStruct(x.shape, bf16),
        in_specs=[hbm] * 5 + [vmem] + [hbm] * len(so_far),
        input_output_aliases={6: 0} if so_far else {},
        out_specs=hbm,
        scratch_shapes=[
            pltpu.VMEM((PART_GROUPS, TOK, GROUP_COLS), bf16),
            pltpu.VMEM((TOK, HEADS), f32),
            pltpu.VMEM((TOK, HEADS), f32),
            pltpu.VMEM((TOK, GROUPS * STATE), bf16),
            pltpu.VMEM((TOK, GROUPS * STATE), bf16),
            pltpu.VMEM((PART_GROUPS, TOK, GROUP_COLS), bf16),
            pltpu.SemaphoreType.DMA((4,)),
            pltpu.SemaphoreType.DMA((PART_GROUPS,)),
            pltpu.SemaphoreType.DMA((PART_GROUPS,)),
        ],
        compiler_params=pltpu.CompilerParams(vmem_limit_bytes=VMEM_LIMIT),
        cost_estimate=pl.CostEstimate(
            flops=2_000_000_000, bytes_accessed=6_000_000, transcendentals=65536
        ),
        name=f"local{part}",
    )(x, step, decay, inject, readout, gain, *so_far)


def out_kernel(
    decay_hbm, readout_hbm, held_ref, local_hbm, out_hbm,
    decay_buf, readout_buf, local_buf, out_buf, sem, local_sem, out_sem,
):
    decay_in, readout_in = copies(
        (decay_hbm, decay_buf, sem.at[0]), (readout_hbm, readout_buf, sem.at[1])
    )
    local_in = copies(
        *[
            (local_hbm.at[:, pl.ds(g * GROUP_COLS, GROUP_COLS)], local_buf.at[g], local_sem.at[g])
            for g in range(GROUPS)
        ]
    )
    lower = jnp.where(iota((TOK, TOK), 0) >= iota((TOK, TOK), 1), 1.0, 0.0).astype(f32)
    decay_in.wait()
    lead = jnp.exp(dot_exact(lower, decay_buf[...]))
    readout_in.wait()
    sent = []
    for g in range(GROUPS):
        readout = readout_buf[:, g * STATE : (g + 1) * STATE]
        local_in[g].wait()
        for k in range(GROUP_COLS // WIDE):
            cols = slice(k * WIDE, (k + 1) * WIDE)
            at = g * GROUP_COLS + k * WIDE
            first = at // COLS
            held = jnp.concatenate(
                [held_ref[first + i] for i in range(WIDE // COLS)], axis=1
            )
            out = dot(readout, held) * spread(lead, at, WIDE) + local_buf[g, :, cols].astype(f32)
            out_buf[g, :, cols] = out.astype(bf16)
        sent += copies(
            (out_buf.at[g], out_hbm.at[:, pl.ds(g * GROUP_COLS, GROUP_COLS)], out_sem.at[g])
        )
    for c in sent:
        c.wait()


def outputs_of(decay, readout, held, local):
    hbm = pl.BlockSpec(memory_space=pltpu.HBM)
    vmem = pl.BlockSpec(memory_space=pltpu.VMEM)
    return pl.pallas_call(
        out_kernel,
        out_shape=jax.ShapeDtypeStruct((TOK, HEADS * HEAD_DIM), bf16),
        in_specs=[hbm, hbm, vmem, hbm],
        out_specs=hbm,
        scratch_shapes=[
            pltpu.VMEM((TOK, HEADS), f32),
            pltpu.VMEM((TOK, GROUPS * STATE), bf16),
            pltpu.VMEM((GROUPS, TOK, GROUP_COLS), bf16),
            pltpu.VMEM((GROUPS, TOK, GROUP_COLS), bf16),
            pltpu.SemaphoreType.DMA((2,)),
            pltpu.SemaphoreType.DMA((GROUPS,)),
            pltpu.SemaphoreType.DMA((GROUPS,)),
        ],
        compiler_params=pltpu.CompilerParams(vmem_limit_bytes=OUT_VMEM_LIMIT),
        cost_estimate=pl.CostEstimate(
            flops=2_000_000_000, bytes_accessed=12_000_000, transcendentals=32768
        ),
        name="outputs",
    )(decay, readout, held, local)


def later_by(v, shift, ways):
    return lax.ppermute(v, "seq", [(i, i + shift) for i in range(ways - shift)])


def exchange(v, devices):
    return lax.all_to_all(
        v,
        ("seq", "head"),
        split_axis=0,
        concat_axis=0,
        tiled=True,
        axis_index_groups=[
            list(range(first, first + OWNERS)) for first in range(0, devices, OWNERS)
        ],
    )


def shards(features, step_size, log_decay, inject, readout, skip_gain):
    ways = lax.axis_size("seq")
    devices = ways * lax.axis_size("head")
    args = (features, step_size, log_decay, inject, readout, skip_gain[None, :])
    arrived = exchange(states_of(features, step_size, log_decay, inject), devices)
    local = local_of(0, (), *args)
    arrived, local = lax.optimization_barrier((arrived, local))
    total = total_of(arrived)
    earlier = [later_by(total, k * STEP, ways) for k in (1, 2, 3)]
    held = held_of(earlier, arrived)
    held = exchange(held, devices)
    local = local_of(1, (local,), *args)
    return outputs_of(log_decay, readout, held, local)


def solution(mesh):
    rows = P(("seq", "head"), None)
    return jax.shard_map(
        shards,
        mesh=mesh,
        in_specs=(rows, rows, rows, rows, rows, P()),
        out_specs=rows,
        check_vma=False,
    )
```

```python
import functools

import jax
import jax.numpy as jnp
from jax import lax
from jax.experimental import pallas as pl
from jax.experimental.pallas import tpu as pltpu
from jax.sharding import PartitionSpec as P

HEADS = 128
HEAD_DIM = 64
STATE = 128
GROUPS = 8
GROUP_HEADS = HEADS // GROUPS
TOK = 256
HALF = 128
LANES = 128
PARTS = 2
PART_GROUPS = GROUPS // PARTS
GROUP_COLS = GROUP_HEADS * HEAD_DIM
PART_COLS = PART_GROUPS * GROUP_COLS
OWNERS = HEADS // PARTS
STEP = 4
ROWS = STATE // 2
EXTRA = 8
WIDE = 512
VMEM_LIMIT = 61 * 1024 * 1024
OUT_VMEM_LIMIT = 50 * 1024 * 1024
HELD_VMEM_LIMIT = 40 * 1024 * 1024
SMALL_VMEM_LIMIT = 24 * 1024 * 1024

f32 = jnp.float32
bf16 = jnp.bfloat16


def dot(a, b):
    return jnp.dot(a, b, preferred_element_type=f32)


def dot_exact(a, b):
    return jnp.dot(a, b, preferred_element_type=f32, precision=lax.Precision.HIGHEST)


def iota(shape, axis):
    return lax.broadcasted_iota(jnp.int32, shape, axis)


def spread(scale, first_col, cols):
    place = iota((scale.shape[0], LANES), 1) >> 6
    first_head = first_col // HEAD_DIM
    return jnp.concatenate(
        [
            jnp.take_along_axis(
                scale, place + (first_head + 2 * k), axis=1, mode="promise_in_bounds"
            )
            for k in range(cols // LANES)
        ],
        axis=1,
    )


def copies(*triples):
    made = [pltpu.make_async_copy(*t) for t in triples]
    for c in made:
        c.start()
    return made


def swap_matrix():
    row = iota((2 * LANES, 2 * LANES), 0)
    quarter = row >> 6
    goal = jnp.where(quarter == 1, 2, jnp.where(quarter == 2, 1, quarter))
    hit = iota((2 * LANES, 2 * LANES), 1) == goal * HEAD_DIM + (row & (HEAD_DIM - 1))
    return jnp.where(hit, 1.0, 0.0).astype(bf16)


def state_kernel(
    part, x_hbm, step_hbm, decay_hbm, inject_hbm, out_hbm,
    x_buf, step_buf, decay_buf, inject_buf, out_buf, sem, in_sem, out_sem,
):
    decay_in, step_in, inject_in = copies(
        (decay_hbm, decay_buf, sem.at[0]),
        (step_hbm, step_buf, sem.at[1]),
        (inject_hbm.at[:, pl.ds(part * PART_GROUPS * STATE, PART_GROUPS * STATE)], inject_buf, sem.at[2]),
    )
    x_in = copies(
        *[
            (
                x_hbm.at[:, pl.ds(part * PART_COLS + n * GROUP_COLS, GROUP_COLS)],
                x_buf.at[n],
                in_sem.at[n],
            )
            for n in range(PART_GROUPS)
        ]
    )
    swap = swap_matrix()
    later = jnp.where(iota((TOK, TOK), 1) > iota((TOK, TOK), 0), 1.0, 0.0).astype(f32)
    decay_in.wait()
    decay = decay_buf[...]
    tail = dot_exact(later, decay)
    if part == 0:
        whole = jnp.broadcast_to(jnp.exp(tail[0:1] + decay[0:1]), (EXTRA, HEADS))
        other = jnp.concatenate([whole[:, OWNERS:], whole[:, :OWNERS]], axis=1)
        row = iota((EXTRA, HEADS), 0)
        value = jnp.where(row < 2, whole, jnp.where(row < 4, other, 0.0))
        high = value.astype(bf16).astype(f32)
        extra = jnp.where((row & 1) == 0, high, value - high)
    step_in.wait()
    scale = step_buf[...] * jnp.exp(tail)
    inject_in.wait()
    sent = []
    for n in range(PART_GROUPS):
        g = part * PART_GROUPS + n
        weight = spread(scale, g * GROUP_COLS, GROUP_COLS)
        x_in[n].wait()
        v = (x_buf[n].astype(f32) * weight).astype(bf16)
        s = lax.dot_general(
            inject_buf[:, n * STATE : (n + 1) * STATE],
            v,
            (((0,), (0,)), ((), ())),
            preferred_element_type=f32,
        ).astype(bf16)
        pairs = jnp.concatenate(
            [
                jnp.concatenate([s[:ROWS, k * LANES : (k + 1) * LANES], s[ROWS:, k * LANES : (k + 1) * LANES]], axis=1)
                for k in range(GROUP_COLS // LANES)
            ],
            axis=0,
        )
        blocks = dot(pairs, swap).astype(bf16)
        first = n * GROUP_HEADS
        for k in range(GROUP_HEADS):
            top = k // 2 * ROWS
            left = k % 2 * LANES
            out_buf[first + k, :ROWS, :] = blocks[top : top + ROWS, left : left + LANES]
            if part == 0:
                place = jnp.full((EXTRA, LANES), first + k, jnp.int32)
                out_buf[first + k, ROWS:, :] = jnp.take_along_axis(
                    extra, place, axis=1, mode="promise_in_bounds"
                ).astype(bf16)
        span = pl.ds(first, GROUP_HEADS)
        sent += copies((out_buf.at[span], out_hbm.at[span], out_sem.at[n]))
    for c in sent:
        c.wait()


def states_of(part, x, step, decay, inject):
    hbm = pl.BlockSpec(memory_space=pltpu.HBM)
    shape = (OWNERS, ROWS + (EXTRA if part == 0 else 0), LANES)
    return pl.pallas_call(
        functools.partial(state_kernel, part),
        out_shape=jax.ShapeDtypeStruct(shape, bf16),
        in_specs=[hbm] * 4,
        out_specs=hbm,
        scratch_shapes=[
            pltpu.VMEM((PART_GROUPS, TOK, GROUP_COLS), bf16),
            pltpu.VMEM((TOK, HEADS), f32),
            pltpu.VMEM((TOK, HEADS), f32),
            pltpu.VMEM((TOK, PART_GROUPS * STATE), bf16),
            pltpu.VMEM(shape, bf16),
            pltpu.SemaphoreType.DMA((3,)),
            pltpu.SemaphoreType.DMA((PART_GROUPS,)),
            pltpu.SemaphoreType.DMA((PART_GROUPS,)),
        ],
        compiler_params=pltpu.CompilerParams(vmem_limit_bytes=VMEM_LIMIT),
        cost_estimate=pl.CostEstimate(
            flops=1_000_000_000, bytes_accessed=4_000_000, transcendentals=32768
        ),
        name=f"states{part}",
    )(x, step, decay, inject)


def two_rows(block, at):
    return block[at : at + 1].astype(f32) + block[at + 1 : at + 2].astype(f32)


def total_kernel(part, in_ref, decay_ref, out_ref):
    state = jnp.zeros((ROWS, LANES), f32)
    decay = jnp.ones((1, LANES), f32)
    for i in range(OWNERS):
        d = two_rows(decay_ref[i, ROWS:, :], 2 * part)
        state = state * d + in_ref[i, :ROWS, :].astype(f32)
        decay = decay * d
    out_ref[:ROWS, :] = state.astype(bf16)
    row = iota((EXTRA, LANES), 0)
    high = decay.astype(bf16).astype(f32)
    rows = jnp.where(row == 0, high, jnp.where(row == 1, decay - high, 0.0))
    out_ref[ROWS:, :] = rows.astype(bf16)


def held_kernel(part, one_ref, two_ref, three_ref, in_ref, decay_ref, out_hbm, out_buf, sem):
    state = three_ref[:ROWS, :].astype(f32)
    for ref in (two_ref, one_ref):
        state = ref[:ROWS, :].astype(f32) + two_rows(ref[ROWS:, :], 0) * state
    sent = []
    for i in range(OWNERS):
        out_buf[i] = state.astype(bf16)
        if (i + 1) % GROUP_HEADS == 0:
            span = pl.ds(i + 1 - GROUP_HEADS, GROUP_HEADS)
            sent += copies((out_buf.at[span], out_hbm.at[span], sem.at[i // GROUP_HEADS]))
        if i + 1 < OWNERS:
            d = two_rows(decay_ref[i, ROWS:, :], 2 * part)
            state = state * d + in_ref[i, :ROWS, :].astype(f32)
    for c in sent:
        c.wait()


def total_of(part, arrived, decays):
    return pl.pallas_call(
        functools.partial(total_kernel, part),
        out_shape=jax.ShapeDtypeStruct((ROWS + EXTRA, LANES), bf16),
        compiler_params=pltpu.CompilerParams(vmem_limit_bytes=SMALL_VMEM_LIMIT),
        cost_estimate=pl.CostEstimate(flops=2_000_000, bytes_accessed=1_000_000, transcendentals=0),
        name=f"total{part}",
    )(arrived, decays)


def held_of(part, earlier, arrived, decays):
    vmem = pl.BlockSpec(memory_space=pltpu.VMEM)
    return pl.pallas_call(
        functools.partial(held_kernel, part),
        out_shape=jax.ShapeDtypeStruct((OWNERS, ROWS, LANES), bf16),
        in_specs=[vmem] * 5,
        out_specs=pl.BlockSpec(memory_space=pltpu.HBM),
        scratch_shapes=[
            pltpu.VMEM((OWNERS, ROWS, LANES), bf16),
            pltpu.SemaphoreType.DMA((OWNERS // GROUP_HEADS,)),
        ],
        compiler_params=pltpu.CompilerParams(vmem_limit_bytes=HELD_VMEM_LIMIT),
        cost_estimate=pl.CostEstimate(flops=2_000_000, bytes_accessed=2_000_000, transcendentals=0),
        name=f"held{part}",
    )(*earlier, arrived, decays)


def local_kernel(
    part, x_hbm, step_hbm, decay_hbm, inject_hbm, readout_hbm, gain_ref, out_hbm,
    x_buf, step_buf, decay_buf, inject_buf, readout_buf, out_buf, sem, in_sem, out_sem,
):
    decay_in, step_in, inject_in, readout_in = copies(
        (decay_hbm, decay_buf, sem.at[0]),
        (step_hbm, step_buf, sem.at[1]),
        (inject_hbm, inject_buf, sem.at[2]),
        (readout_hbm, readout_buf, sem.at[3]),
    )
    x_in = copies(
        *[
            (
                x_hbm.at[:, pl.ds(part * PART_COLS + n * GROUP_COLS, GROUP_COLS)],
                x_buf.at[n],
                in_sem.at[n],
            )
            for n in range(PART_GROUPS)
        ]
    )
    lower = iota((HALF, HALF), 0) >= iota((HALF, HALF), 1)
    lower_f = jnp.where(lower, 1.0, 0.0).astype(f32)
    decay_in.wait()
    cum_a = dot_exact(lower_f, decay_buf[:HALF])
    cum_b = dot_exact(lower_f, decay_buf[HALF:])
    mid = HALF // 2 - 1
    mid_b = cum_b[mid : mid + 1]
    gap_a = cum_a - cum_a[mid : mid + 1]
    gap_b = cum_b - mid_b
    onward = jnp.exp(mid_b + gap_a[HALF - 1 : HALF])
    few = iota((8, HEADS), 0)
    rows = jnp.where(few == 0, onward, gain_ref[...])
    step_in.wait()
    into_a = step_buf[:HALF] * jnp.exp(-gap_a)
    into_b = step_buf[HALF:] * jnp.exp(-gap_b)
    from_a = jnp.exp(gap_a)
    from_b = jnp.exp(gap_b)
    zero = jnp.zeros((HALF, HALF), f32)
    inject_in.wait()
    readout_in.wait()

    def pair(r, i):
        return lax.dot_general(r, i, (((1,), (1,)), ((), ())), preferred_element_type=f32)

    sent = []
    for n in range(PART_GROUPS):
        g = part * PART_GROUPS + n
        state_cols = slice(g * STATE, (g + 1) * STATE)
        inj_a = inject_buf[:HALF, state_cols]
        inj_b = inject_buf[HALF:, state_cols]
        read_a = readout_buf[:HALF, state_cols]
        read_b = readout_buf[HALF:, state_cols]
        near_a = jnp.where(lower, pair(read_a, inj_a), zero).astype(bf16)
        near_b = jnp.concatenate(
            [
                pair(read_b, inj_a).astype(bf16),
                jnp.where(lower, pair(read_b, inj_b), zero).astype(bf16),
            ],
            axis=1,
        )
        x_in[n].wait()
        for k in range(GROUP_COLS // WIDE):
            cols = slice(k * WIDE, (k + 1) * WIDE)
            at = g * GROUP_COLS + k * WIDE
            row = spread(rows, at, WIDE)
            gain = row[1:2]
            x_a = x_buf[n, :HALF, cols].astype(f32)
            x_b = x_buf[n, HALF:, cols].astype(f32)
            v_a = x_a * spread(into_a, at, WIDE)
            v_b = (x_b * spread(into_b, at, WIDE)).astype(bf16)
            res_a = dot(near_a, v_a.astype(bf16))
            res_b = dot(near_b, jnp.concatenate([(v_a * row[0:1]).astype(bf16), v_b], axis=0))
            out_a = res_a * spread(from_a, at, WIDE) + gain * x_a
            out_b = res_b * spread(from_b, at, WIDE) + gain * x_b
            out_buf[n, :HALF, cols] = out_a.astype(bf16)
            out_buf[n, HALF:, cols] = out_b.astype(bf16)
        sent += copies(
            (out_buf.at[n], out_hbm.at[:, pl.ds(g * GROUP_COLS, GROUP_COLS)], out_sem.at[n])
        )
    for c in sent:
        c.wait()


def local_of(part, x, step, decay, inject, readout, gain):
    hbm = pl.BlockSpec(memory_space=pltpu.HBM)
    vmem = pl.BlockSpec(memory_space=pltpu.VMEM)
    return pl.pallas_call(
        functools.partial(local_kernel, part),
        out_shape=jax.ShapeDtypeStruct(x.shape, bf16),
        in_specs=[hbm] * 5 + [vmem],
        out_specs=hbm,
        scratch_shapes=[
            pltpu.VMEM((PART_GROUPS, TOK, GROUP_COLS), bf16),
            pltpu.VMEM((TOK, HEADS), f32),
            pltpu.VMEM((TOK, HEADS), f32),
            pltpu.VMEM((TOK, GROUPS * STATE), bf16),
            pltpu.VMEM((TOK, GROUPS * STATE), bf16),
            pltpu.VMEM((PART_GROUPS, TOK, GROUP_COLS), bf16),
            pltpu.SemaphoreType.DMA((4,)),
            pltpu.SemaphoreType.DMA((PART_GROUPS,)),
            pltpu.SemaphoreType.DMA((PART_GROUPS,)),
        ],
        compiler_params=pltpu.CompilerParams(vmem_limit_bytes=VMEM_LIMIT),
        cost_estimate=pl.CostEstimate(
            flops=2_000_000_000, bytes_accessed=6_000_000, transcendentals=65536
        ),
        name=f"local{part}",
    )(x, step, decay, inject, readout, gain)


def out_kernel(part, decay_hbm, readout_hbm, held_ref, local_hbm, *rest):
    out_hbm, decay_buf, readout_buf, local_buf, out_buf, sem, local_sem, out_sem = rest[-8:]
    decay_in, readout_in = copies(
        (decay_hbm, decay_buf, sem.at[0]),
        (
            readout_hbm.at[:, pl.ds(part * PART_GROUPS * STATE, PART_GROUPS * STATE)],
            readout_buf,
            sem.at[1],
        ),
    )
    local_in = copies(
        *[
            (
                local_hbm.at[:, pl.ds(part * PART_COLS + n * GROUP_COLS, GROUP_COLS)],
                local_buf.at[n],
                local_sem.at[n],
            )
            for n in range(PART_GROUPS)
        ]
    )
    swap = swap_matrix()
    lower = jnp.where(iota((TOK, TOK), 0) >= iota((TOK, TOK), 1), 1.0, 0.0).astype(f32)
    decay_in.wait()
    lead = jnp.exp(dot_exact(lower, decay_buf[...]))
    readout_in.wait()
    sent = []
    for n in range(PART_GROUPS):
        g = part * PART_GROUPS + n
        first = n * GROUP_HEADS
        blocks = jnp.concatenate(
            [
                jnp.concatenate([held_ref[first + k], held_ref[first + k + 1]], axis=1)
                for k in range(0, GROUP_HEADS, 2)
            ],
            axis=0,
        )
        pairs = dot(blocks, swap).astype(bf16)
        readout = readout_buf[:, n * STATE : (n + 1) * STATE]
        local_in[n].wait()
        for k in range(GROUP_COLS // WIDE):
            cols = slice(k * WIDE, (k + 1) * WIDE)
            tiles = range(k * WIDE // LANES, (k + 1) * WIDE // LANES)
            held = jnp.concatenate(
                [
                    jnp.concatenate([pairs[i * ROWS : (i + 1) * ROWS, side] for i in tiles], axis=1)
                    for side in (slice(0, LANES), slice(LANES, 2 * LANES))
                ],
                axis=0,
            )
            far = dot(readout, held) * spread(lead, g * GROUP_COLS + k * WIDE, WIDE)
            out_buf[n, :, cols] = (far + local_buf[n, :, cols].astype(f32)).astype(bf16)
        sent += copies(
            (out_buf.at[n], out_hbm.at[:, pl.ds(g * GROUP_COLS, GROUP_COLS)], out_sem.at[n])
        )
    for c in sent:
        c.wait()


def outputs_of(part, so_far, decay, readout, held, local):
    hbm = pl.BlockSpec(memory_space=pltpu.HBM)
    vmem = pl.BlockSpec(memory_space=pltpu.VMEM)
    return pl.pallas_call(
        functools.partial(out_kernel, part),
        out_shape=jax.ShapeDtypeStruct((TOK, HEADS * HEAD_DIM), bf16),
        in_specs=[hbm, hbm, vmem, hbm] + [hbm] * len(so_far),
        out_specs=hbm,
        input_output_aliases={4: 0} if so_far else {},
        scratch_shapes=[
            pltpu.VMEM((TOK, HEADS), f32),
            pltpu.VMEM((TOK, PART_GROUPS * STATE), bf16),
            pltpu.VMEM((PART_GROUPS, TOK, GROUP_COLS), bf16),
            pltpu.VMEM((PART_GROUPS, TOK, GROUP_COLS), bf16),
            pltpu.SemaphoreType.DMA((2,)),
            pltpu.SemaphoreType.DMA((PART_GROUPS,)),
            pltpu.SemaphoreType.DMA((PART_GROUPS,)),
        ],
        compiler_params=pltpu.CompilerParams(vmem_limit_bytes=OUT_VMEM_LIMIT),
        cost_estimate=pl.CostEstimate(
            flops=1_000_000_000, bytes_accessed=6_000_000, transcendentals=32768
        ),
        name=f"outputs{part}",
    )(decay, readout, held, local, *so_far)


def later_by(v, shift, ways):
    return lax.ppermute(v, "seq", [(i, i + shift) for i in range(ways - shift)])


def exchange(v, devices):
    return lax.all_to_all(
        v,
        ("seq", "head"),
        split_axis=0,
        concat_axis=0,
        tiled=True,
        axis_index_groups=[
            list(range(first, first + OWNERS)) for first in range(0, devices, OWNERS)
        ],
    )


def shards(features, step_size, log_decay, inject, readout, skip_gain):
    ways = lax.axis_size("seq")
    devices = ways * lax.axis_size("head")
    args = (features, step_size, log_decay, inject, readout, skip_gain[None, :])

    def hold(part, arrived, decays):
        total = total_of(part, arrived, decays)
        earlier = [later_by(total, k * STEP, ways) for k in (1, 2, 3)]
        return held_of(part, earlier, arrived, decays)

    arrived_0 = exchange(states_of(0, features, step_size, log_decay, inject), devices)
    states_1 = states_of(1, features, step_size, log_decay, inject)
    local_0 = local_of(0, *args)
    arrived_0, states_1, local_0 = lax.optimization_barrier((arrived_0, states_1, local_0))
    arrived_1 = exchange(states_1, devices)
    held_0 = hold(0, arrived_0, arrived_0)
    arrived_1, held_0 = lax.optimization_barrier((arrived_1, held_0))
    back_0 = exchange(held_0, devices)
    held_1 = hold(1, arrived_1, arrived_0)
    back_0, held_1, args = lax.optimization_barrier((back_0, held_1, args))
    back_1 = exchange(held_1, devices)
    local_1 = local_of(1, *args)
    out = outputs_of(0, (), log_decay, readout, back_0, local_0)
    return outputs_of(1, (out,), log_decay, readout, back_1, local_1)


def solution(mesh):
    rows = P(("seq", "head"), None)
    return jax.shard_map(
        shards,
        mesh=mesh,
        in_specs=(rows, rows, rows, rows, rows, P()),
        out_specs=rows,
        check_vma=False,
    )
```

```python
import functools

import jax
import jax.numpy as jnp
from jax import lax
from jax.experimental import pallas as pl
from jax.experimental.pallas import tpu as pltpu
from jax.sharding import PartitionSpec as P

HEADS = 128
HEAD_DIM = 64
STATE = 128
GROUPS = 8
TOK = 256
HALF = 128
LANES = 128
OWNERS = 64
STEP = 4
SPANS = 4
PIECES = 4
OWN_HEADS = HEADS // OWNERS
COLS = OWN_HEADS * HEAD_DIM
GROUP_COLS = HEADS // GROUPS * HEAD_DIM
GROUP_OWNERS = OWNERS // GROUPS
ROWS = STATE + 8
VMEM_LIMIT = 61 * 1024 * 1024
OUT_VMEM_LIMIT = 50 * 1024 * 1024
HELD_VMEM_LIMIT = 52 * 1024 * 1024
SMALL_VMEM_LIMIT = 24 * 1024 * 1024
WIDE = 512
NARROW = 256
LOCAL_PARTS = 2
PART_GROUPS = GROUPS // LOCAL_PARTS
PART_COLS = PART_GROUPS * GROUP_COLS

f32 = jnp.float32
bf16 = jnp.bfloat16


def dot(a, b):
    return jnp.dot(a, b, preferred_element_type=f32)


def sums(mask, v):
    high = v.astype(bf16)
    rest = v - high.astype(f32)
    middle = rest.astype(bf16)
    low = (rest - middle.astype(f32)).astype(bf16)
    p = dot(mask.astype(bf16), jnp.concatenate([high, middle, low], axis=1))
    return p[:, :HEADS] + p[:, HEADS : 2 * HEADS] + p[:, 2 * HEADS :]


def iota(shape, axis):
    return lax.broadcasted_iota(jnp.int32, shape, axis)


def spread(scale, first_col, cols):
    place = iota((scale.shape[0], LANES), 1) >> 6
    first_head = first_col // HEAD_DIM
    return jnp.concatenate(
        [
            jnp.take_along_axis(
                scale, place + (first_head + 2 * k), axis=1, mode="promise_in_bounds"
            )
            for k in range(cols // LANES)
        ],
        axis=1,
    )


def copies(*triples):
    made = [pltpu.make_async_copy(*t) for t in triples]
    for c in made:
        c.start()
    return made


def state_kernel(
    x_hbm, step_hbm, decay_hbm, inject_hbm, out_hbm,
    x_buf, step_buf, decay_buf, inject_buf, turned_buf, v_buf, out_buf, sem, in_sem, out_sem,
):
    decay_in, step_in, inject_in = copies(
        (decay_hbm, decay_buf, sem.at[0]),
        (step_hbm, step_buf, sem.at[1]),
        (inject_hbm, inject_buf, sem.at[2]),
    )
    x_in = copies(
        *[
            (x_hbm.at[:, pl.ds(g * GROUP_COLS, GROUP_COLS)], x_buf.at[g], in_sem.at[g])
            for g in range(GROUPS)
        ]
    )
    later = jnp.where(iota((TOK, TOK), 1) > iota((TOK, TOK), 0), 1.0, 0.0).astype(f32)
    decay_in.wait()
    decay = decay_buf[...]
    tail = sums(later, decay)
    whole = jnp.broadcast_to(jnp.exp(tail[0:1] + decay[0:1]), (8, HEADS))
    high = whole.astype(bf16).astype(f32)
    row = iota((8, HEADS), 0)
    extra = jnp.where(row == 0, high, jnp.where(row == 1, whole - high, 0.0))
    step_in.wait()
    scale = step_buf[...] * jnp.exp(tail)
    inject_in.wait()
    for g in range(GROUPS):
        turned_buf[g] = inject_buf[:, g * STATE : (g + 1) * STATE].T
    sent = []
    for g in range(GROUPS + 1):
        if g < GROUPS:
            if g % 2 == 0:
                x_in[g].wait()
                x_in[g + 1].wait()
        first = (g - 1) * GROUP_OWNERS
        for w in range(GROUP_COLS // NARROW):
            part = slice(w * NARROW, (w + 1) * NARROW)
            if g < GROUPS:
                weight = spread(scale, g * GROUP_COLS + w * NARROW, NARROW)
                v_buf[g % 2, :, part] = (x_buf[g, :, part].astype(f32) * weight).astype(bf16)
            if g > 0:
                s = dot(turned_buf[g - 1], v_buf[(g - 1) % 2, :, part]).astype(bf16)
                below = spread(extra, (g - 1) * GROUP_COLS + w * NARROW, NARROW).astype(bf16)
                for k in range(NARROW // COLS):
                    cols = slice(k * COLS, (k + 1) * COLS)
                    owner = first + w * (NARROW // COLS) + k
                    out_buf[owner, :STATE, :] = s[:, cols]
                    out_buf[owner, STATE:, :] = below[:, cols]
        if g > 0:
            span = pl.ds(first, GROUP_OWNERS)
            sent += copies((out_buf.at[span], out_hbm.at[span], out_sem.at[g - 1]))
    for c in sent:
        c.wait()


def states_of(x, step, decay, inject):
    hbm = pl.BlockSpec(memory_space=pltpu.HBM)
    return pl.pallas_call(
        state_kernel,
        out_shape=jax.ShapeDtypeStruct((OWNERS, ROWS, COLS), bf16),
        in_specs=[hbm] * 4,
        out_specs=hbm,
        scratch_shapes=[
            pltpu.VMEM((GROUPS, TOK, GROUP_COLS), bf16),
            pltpu.VMEM((TOK, HEADS), f32),
            pltpu.VMEM((TOK, HEADS), f32),
            pltpu.VMEM((TOK, GROUPS * STATE), bf16),
            pltpu.VMEM((GROUPS, STATE, TOK), bf16),
            pltpu.VMEM((2, TOK, GROUP_COLS), bf16),
            pltpu.VMEM((OWNERS, ROWS, COLS), bf16),
            pltpu.SemaphoreType.DMA((3,)),
            pltpu.SemaphoreType.DMA((GROUPS,)),
            pltpu.SemaphoreType.DMA((GROUPS,)),
        ],
        compiler_params=pltpu.CompilerParams(vmem_limit_bytes=VMEM_LIMIT),
        cost_estimate=pl.CostEstimate(
            flops=2_000_000_000, bytes_accessed=8_000_000, transcendentals=32768
        ),
        name="states",
    )(x, step, decay, inject)


def decay_row(block):
    return block[STATE : STATE + 1].astype(f32) + block[STATE + 1 : STATE + 2].astype(f32)


def pack_rows(decay):
    row = iota((8, COLS), 0)
    high = decay.astype(bf16).astype(f32)
    return jnp.where(row == 0, high, jnp.where(row == 1, decay - high, 0.0)).astype(bf16)


def total_kernel(place_ref, in_ref, out_ref):
    state = in_ref[0, :STATE, :].astype(f32)
    decay = decay_row(in_ref[0])
    for i in range(1, OWNERS):
        d = decay_row(in_ref[i])
        state = state * d + in_ref[i, :STATE, :].astype(f32)
        decay = decay * d
    rows = pack_rows(decay).astype(f32)
    same = jnp.where(iota((8, COLS), 0) == 0, 1.0, 0.0)
    for k in range(SPANS):
        later = place_ref[0] < k
        out_ref[k, :STATE, :] = jnp.where(later, state, 0.0).astype(bf16)
        out_ref[k, STATE:, :] = jnp.where(later, rows, same).astype(bf16)


def held_kernel(earlier_ref, in_hbm, out_hbm, in_buf, out_buf, in_sem, out_sem):
    size = OWNERS // PIECES
    spans = [pl.ds(i * size, size) for i in range(PIECES)]
    arrive = copies(*[(in_hbm.at[p], in_buf.at[p], in_sem.at[i]) for i, p in enumerate(spans)])
    state = jnp.zeros((STATE, COLS), f32)
    for k in range(SPANS - 1):
        state = earlier_ref[k, :STATE, :].astype(f32) + decay_row(earlier_ref[k]) * state
    sent = []
    for i in range(OWNERS):
        if i % size == 0:
            arrive[i // size].wait()
        out_buf[i] = state.astype(bf16)
        if (i + 1) % size == 0:
            p = spans[i // size]
            sent += copies((out_buf.at[p], out_hbm.at[p], out_sem.at[i // size]))
        if i + 1 < OWNERS:
            state = state * decay_row(in_buf[i]) + in_buf[i, :STATE, :].astype(f32)
    for c in sent:
        c.wait()


def total_of(place, arrived):
    return pl.pallas_call(
        total_kernel,
        out_shape=jax.ShapeDtypeStruct((SPANS, ROWS, COLS), bf16),
        in_specs=[
            pl.BlockSpec(memory_space=pltpu.SMEM),
            pl.BlockSpec(memory_space=pltpu.VMEM),
        ],
        compiler_params=pltpu.CompilerParams(vmem_limit_bytes=SMALL_VMEM_LIMIT),
        cost_estimate=pl.CostEstimate(flops=4_000_000, bytes_accessed=2_000_000, transcendentals=0),
        name="total",
    )(place, arrived)


def held_of(earlier, arrived):
    hbm = pl.BlockSpec(memory_space=pltpu.HBM)
    return pl.pallas_call(
        held_kernel,
        out_shape=jax.ShapeDtypeStruct((OWNERS, STATE, COLS), bf16),
        in_specs=[pl.BlockSpec(memory_space=pltpu.VMEM), hbm],
        out_specs=hbm,
        scratch_shapes=[
            pltpu.VMEM((OWNERS, ROWS, COLS), bf16),
            pltpu.VMEM((OWNERS, STATE, COLS), bf16),
            pltpu.SemaphoreType.DMA((PIECES,)),
            pltpu.SemaphoreType.DMA((PIECES,)),
        ],
        compiler_params=pltpu.CompilerParams(vmem_limit_bytes=HELD_VMEM_LIMIT),
        cost_estimate=pl.CostEstimate(flops=4_000_000, bytes_accessed=4_000_000, transcendentals=0),
        name="held",
    )(earlier, arrived)


def local_kernel(
    part, x_hbm, step_hbm, decay_hbm, inject_hbm, readout_hbm, gain_ref, *rest
):
    if part == 0:
        out_hbm, lead_ref = rest[:2]
    else:
        out_hbm = rest[1]
    x_buf, step_buf, decay_buf, inject_buf, readout_buf, out_buf, sem, in_sem, out_sem = rest[2:]
    decay_in, step_in, inject_in, readout_in = copies(
        (decay_hbm, decay_buf, sem.at[0]),
        (step_hbm, step_buf, sem.at[1]),
        (inject_hbm, inject_buf, sem.at[2]),
        (readout_hbm, readout_buf, sem.at[3]),
    )
    x_in = copies(
        *[
            (
                x_hbm.at[:, pl.ds(part * PART_COLS + n * GROUP_COLS, GROUP_COLS)],
                x_buf.at[n],
                in_sem.at[n],
            )
            for n in range(PART_GROUPS)
        ]
    )
    lower = iota((HALF, HALF), 0) >= iota((HALF, HALF), 1)
    lower_f = jnp.where(lower, 1.0, 0.0).astype(f32)
    decay_in.wait()
    cum_a = sums(lower_f, decay_buf[:HALF])
    cum_b = sums(lower_f, decay_buf[HALF:])
    if part == 0:
        lead_ref[:HALF] = jnp.exp(cum_a)
        lead_ref[HALF:] = jnp.exp(cum_b + cum_a[HALF - 1 : HALF])
    mid = HALF // 2 - 1
    mid_b = cum_b[mid : mid + 1]
    gap_a = cum_a - cum_a[mid : mid + 1]
    gap_b = cum_b - mid_b
    onward = jnp.exp(mid_b + gap_a[HALF - 1 : HALF])
    few = iota((8, HEADS), 0)
    rows = jnp.where(few == 0, onward, gain_ref[...])
    step_in.wait()
    into_a = step_buf[:HALF] * jnp.exp(-gap_a)
    into_b = step_buf[HALF:] * jnp.exp(-gap_b)
    from_a = jnp.exp(gap_a)
    from_b = jnp.exp(gap_b)
    zero = jnp.zeros((HALF, HALF), f32)
    inject_in.wait()
    readout_in.wait()

    def pair(r, i):
        return lax.dot_general(r, i, (((1,), (1,)), ((), ())), preferred_element_type=f32)

    sent = []
    for n in range(PART_GROUPS):
        g = part * PART_GROUPS + n
        state_cols = slice(g * STATE, (g + 1) * STATE)
        inj_a = inject_buf[:HALF, state_cols]
        inj_b = inject_buf[HALF:, state_cols]
        read_a = readout_buf[:HALF, state_cols]
        read_b = readout_buf[HALF:, state_cols]
        near_a = jnp.where(lower, pair(read_a, inj_a), zero).astype(bf16)
        near_b = jnp.concatenate(
            [
                pair(read_b, inj_a).astype(bf16),
                jnp.where(lower, pair(read_b, inj_b), zero).astype(bf16),
            ],
            axis=1,
        )
        x_in[n].wait()
        for k in range(GROUP_COLS // WIDE):
            cols = slice(k * WIDE, (k + 1) * WIDE)
            at = g * GROUP_COLS + k * WIDE
            row = spread(rows, at, WIDE)
            gain = row[1:2]
            x_a = x_buf[n, :HALF, cols].astype(f32)
            x_b = x_buf[n, HALF:, cols].astype(f32)
            v_a = x_a * spread(into_a, at, WIDE)
            v_b = (x_b * spread(into_b, at, WIDE)).astype(bf16)
            res_a = dot(near_a, v_a.astype(bf16))
            res_b = dot(near_b, jnp.concatenate([(v_a * row[0:1]).astype(bf16), v_b], axis=0))
            out_a = res_a * spread(from_a, at, WIDE) + gain * x_a
            out_b = res_b * spread(from_b, at, WIDE) + gain * x_b
            out_buf[n, :HALF, cols] = out_a.astype(bf16)
            out_buf[n, HALF:, cols] = out_b.astype(bf16)
        sent += copies(
            (out_buf.at[n], out_hbm.at[:, pl.ds(g * GROUP_COLS, GROUP_COLS)], out_sem.at[n])
        )
    for c in sent:
        c.wait()


def local_of(part, so_far, x, step, decay, inject, readout, gain):
    hbm = pl.BlockSpec(memory_space=pltpu.HBM)
    vmem = pl.BlockSpec(memory_space=pltpu.VMEM)
    return pl.pallas_call(
        functools.partial(local_kernel, part),
        out_shape=[jax.ShapeDtypeStruct(x.shape, bf16)]
        + ([] if so_far else [jax.ShapeDtypeStruct((TOK, HEADS), f32)]),
        in_specs=[hbm] * 5 + [vmem] + [hbm] * len(so_far),
        input_output_aliases={6: 0} if so_far else {},
        out_specs=[hbm] if so_far else [hbm, vmem],
        scratch_shapes=[
            pltpu.VMEM((PART_GROUPS, TOK, GROUP_COLS), bf16),
            pltpu.VMEM((TOK, HEADS), f32),
            pltpu.VMEM((TOK, HEADS), f32),
            pltpu.VMEM((TOK, GROUPS * STATE), bf16),
            pltpu.VMEM((TOK, GROUPS * STATE), bf16),
            pltpu.VMEM((PART_GROUPS, TOK, GROUP_COLS), bf16),
            pltpu.SemaphoreType.DMA((4,)),
            pltpu.SemaphoreType.DMA((PART_GROUPS,)),
            pltpu.SemaphoreType.DMA((PART_GROUPS,)),
        ],
        compiler_params=pltpu.CompilerParams(vmem_limit_bytes=VMEM_LIMIT),
        cost_estimate=pl.CostEstimate(
            flops=2_000_000_000, bytes_accessed=6_000_000, transcendentals=65536
        ),
        name=f"local{part}",
    )(x, step, decay, inject, readout, gain, *so_far)


def out_kernel(
    lead_ref, readout_ref, held_ref, local_hbm, out_hbm, far_buf, local_buf, out_buf, local_sem, out_sem
):
    local_in = copies(
        *[
            (local_hbm.at[:, pl.ds(g * GROUP_COLS, GROUP_COLS)], local_buf.at[g], local_sem.at[g])
            for g in range(GROUPS)
        ]
    )
    sent = []
    for g in range(GROUPS + 1):
        if g > 0:
            local_in[g - 1].wait()
        if g < GROUPS:
            held = jnp.concatenate(
                [held_ref[g * GROUP_OWNERS + i] for i in range(GROUP_OWNERS)], axis=1
            )
            far_buf[g % 2] = dot(readout_ref[:, g * STATE : (g + 1) * STATE], held)
        if g > 0:
            at = (g - 1) * GROUP_COLS
            far = far_buf[(g - 1) % 2] * spread(lead_ref[...], at, GROUP_COLS)
            out_buf[g - 1] = (far + local_buf[g - 1].astype(f32)).astype(bf16)
            sent += copies(
                (out_buf.at[g - 1], out_hbm.at[:, pl.ds(at, GROUP_COLS)], out_sem.at[g - 1])
            )
    for c in sent:
        c.wait()


def outputs_of(lead, readout, held, local):
    hbm = pl.BlockSpec(memory_space=pltpu.HBM)
    vmem = pl.BlockSpec(memory_space=pltpu.VMEM)
    return pl.pallas_call(
        out_kernel,
        out_shape=jax.ShapeDtypeStruct((TOK, HEADS * HEAD_DIM), bf16),
        in_specs=[vmem, vmem, vmem, hbm],
        out_specs=hbm,
        scratch_shapes=[
            pltpu.VMEM((2, TOK, GROUP_COLS), f32),
            pltpu.VMEM((GROUPS, TOK, GROUP_COLS), bf16),
            pltpu.VMEM((GROUPS, TOK, GROUP_COLS), bf16),
            pltpu.SemaphoreType.DMA((GROUPS,)),
            pltpu.SemaphoreType.DMA((GROUPS,)),
        ],
        compiler_params=pltpu.CompilerParams(vmem_limit_bytes=OUT_VMEM_LIMIT),
        cost_estimate=pl.CostEstimate(
            flops=2_000_000_000, bytes_accessed=12_000_000, transcendentals=0
        ),
        name="outputs",
    )(lead, readout, held, local)


def across(v, ways):
    return lax.all_to_all(
        v,
        "seq",
        split_axis=0,
        concat_axis=0,
        tiled=True,
        axis_index_groups=[list(range(i, ways, STEP)) for i in range(STEP)],
    )


def exchange(v, devices):
    return lax.all_to_all(
        v,
        ("seq", "head"),
        split_axis=0,
        concat_axis=0,
        tiled=True,
        axis_index_groups=[
            list(range(first, first + OWNERS)) for first in range(0, devices, OWNERS)
        ],
    )


def shards(features, step_size, log_decay, inject, readout, skip_gain):
    ways = lax.axis_size("seq")
    devices = ways * lax.axis_size("head")
    args = (features, step_size, log_decay, inject, readout, skip_gain[None, :])
    arrived = exchange(states_of(features, step_size, log_decay, inject), devices)
    local, lead = local_of(0, (), *args)
    arrived, local, lead = lax.optimization_barrier((arrived, local, lead))
    place = (lax.axis_index("seq") // STEP).astype(jnp.int32)[None]
    earlier = across(total_of(place, arrived), ways)
    held = held_of(earlier, arrived)
    held = exchange(held, devices)
    (local,) = local_of(1, (local,), *args)
    return outputs_of(lead, readout, held, local)


def solution(mesh):
    rows = P(("seq", "head"), None)
    return jax.shard_map(
        shards,
        mesh=mesh,
        in_specs=(rows, rows, rows, rows, rows, P()),
        out_specs=rows,
        check_vma=False,
    )
```

```python
import functools

import jax
import jax.numpy as jnp
from jax import lax
from jax.experimental import pallas as pl
from jax.experimental.pallas import tpu as pltpu
from jax.sharding import PartitionSpec as P

HEADS = 128
HEAD_DIM = 64
STATE = 128
GROUPS = 8
TOK = 256
HALF = 128
LANES = 128
OWNERS = 64
STEP = 4
PIECES = 4
OWN_HEADS = HEADS // OWNERS
COLS = OWN_HEADS * HEAD_DIM
GROUP_COLS = HEADS // GROUPS * HEAD_DIM
GROUP_OWNERS = OWNERS // GROUPS
ROWS = STATE + 8
VMEM_LIMIT = 61 * 1024 * 1024
OUT_VMEM_LIMIT = 50 * 1024 * 1024
HELD_VMEM_LIMIT = 40 * 1024 * 1024
SMALL_VMEM_LIMIT = 24 * 1024 * 1024
WIDE = 512
NARROW = 256
LOCAL_PARTS = 2
PART_GROUPS = GROUPS // LOCAL_PARTS
PART_COLS = PART_GROUPS * GROUP_COLS

f32 = jnp.float32
bf16 = jnp.bfloat16


def dot(a, b):
    return jnp.dot(a, b, preferred_element_type=f32)


def sums(mask, v):
    high = v.astype(bf16)
    rest = v - high.astype(f32)
    middle = rest.astype(bf16)
    low = (rest - middle.astype(f32)).astype(bf16)
    p = dot(mask.astype(bf16), jnp.concatenate([high, middle, low], axis=1))
    return p[:, :HEADS] + p[:, HEADS : 2 * HEADS] + p[:, 2 * HEADS :]


def iota(shape, axis):
    return lax.broadcasted_iota(jnp.int32, shape, axis)


def spread(scale, first_col, cols):
    place = iota((scale.shape[0], LANES), 1) >> 6
    first_head = first_col // HEAD_DIM
    return jnp.concatenate(
        [
            jnp.take_along_axis(
                scale, place + (first_head + 2 * k), axis=1, mode="promise_in_bounds"
            )
            for k in range(cols // LANES)
        ],
        axis=1,
    )


def copies(*triples):
    made = [pltpu.make_async_copy(*t) for t in triples]
    for c in made:
        c.start()
    return made


def state_kernel(
    x_hbm, step_hbm, decay_hbm, inject_hbm, out_hbm,
    x_buf, step_buf, decay_buf, inject_buf, turned_buf, v_buf, out_buf, sem, in_sem, out_sem,
):
    decay_in, step_in, inject_in = copies(
        (decay_hbm, decay_buf, sem.at[0]),
        (step_hbm, step_buf, sem.at[1]),
        (inject_hbm, inject_buf, sem.at[2]),
    )
    x_in = copies(
        *[
            (x_hbm.at[:, pl.ds(g * GROUP_COLS, GROUP_COLS)], x_buf.at[g], in_sem.at[g])
            for g in range(GROUPS)
        ]
    )
    later = jnp.where(iota((TOK, TOK), 1) > iota((TOK, TOK), 0), 1.0, 0.0).astype(f32)
    decay_in.wait()
    decay = decay_buf[...]
    tail = sums(later, decay)
    whole = jnp.broadcast_to(jnp.exp(tail[0:1] + decay[0:1]), (8, HEADS))
    high = whole.astype(bf16).astype(f32)
    row = iota((8, HEADS), 0)
    extra = jnp.where(row == 0, high, jnp.where(row == 1, whole - high, 0.0))
    step_in.wait()
    scale = step_buf[...] * jnp.exp(tail)
    inject_in.wait()
    for g in range(GROUPS):
        turned_buf[g] = inject_buf[:, g * STATE : (g + 1) * STATE].T
    sent = []
    for g in range(GROUPS + 1):
        if g < GROUPS:
            if g % 2 == 0:
                x_in[g].wait()
                x_in[g + 1].wait()
        first = (g - 1) * GROUP_OWNERS
        for w in range(GROUP_COLS // NARROW):
            part = slice(w * NARROW, (w + 1) * NARROW)
            if g < GROUPS:
                weight = spread(scale, g * GROUP_COLS + w * NARROW, NARROW)
                v_buf[g % 2, :, part] = (x_buf[g, :, part].astype(f32) * weight).astype(bf16)
            if g > 0:
                s = dot(turned_buf[g - 1], v_buf[(g - 1) % 2, :, part]).astype(bf16)
                below = spread(extra, (g - 1) * GROUP_COLS + w * NARROW, NARROW).astype(bf16)
                for k in range(NARROW // COLS):
                    cols = slice(k * COLS, (k + 1) * COLS)
                    owner = first + w * (NARROW // COLS) + k
                    out_buf[owner, :STATE, :] = s[:, cols]
                    out_buf[owner, STATE:, :] = below[:, cols]
        if g > 0:
            span = pl.ds(first, GROUP_OWNERS)
            sent += copies((out_buf.at[span], out_hbm.at[span], out_sem.at[g - 1]))
    for c in sent:
        c.wait()


def states_of(x, step, decay, inject):
    hbm = pl.BlockSpec(memory_space=pltpu.HBM)
    return pl.pallas_call(
        state_kernel,
        out_shape=jax.ShapeDtypeStruct((OWNERS, ROWS, COLS), bf16),
        in_specs=[hbm] * 4,
        out_specs=hbm,
        scratch_shapes=[
            pltpu.VMEM((GROUPS, TOK, GROUP_COLS), bf16),
            pltpu.VMEM((TOK, HEADS), f32),
            pltpu.VMEM((TOK, HEADS), f32),
            pltpu.VMEM((TOK, GROUPS * STATE), bf16),
            pltpu.VMEM((GROUPS, STATE, TOK), bf16),
            pltpu.VMEM((2, TOK, GROUP_COLS), bf16),
            pltpu.VMEM((OWNERS, ROWS, COLS), bf16),
            pltpu.SemaphoreType.DMA((3,)),
            pltpu.SemaphoreType.DMA((GROUPS,)),
            pltpu.SemaphoreType.DMA((GROUPS,)),
        ],
        compiler_params=pltpu.CompilerParams(vmem_limit_bytes=VMEM_LIMIT),
        cost_estimate=pl.CostEstimate(
            flops=2_000_000_000, bytes_accessed=8_000_000, transcendentals=32768
        ),
        name="states",
    )(x, step, decay, inject)


def decay_row(block):
    return block[STATE : STATE + 1].astype(f32) + block[STATE + 1 : STATE + 2].astype(f32)


def pack_rows(decay):
    row = iota((8, COLS), 0)
    high = decay.astype(bf16).astype(f32)
    return jnp.where(row == 0, high, jnp.where(row == 1, decay - high, 0.0)).astype(bf16)


def total_kernel(in_ref, out_ref):
    state = in_ref[0, :STATE, :].astype(f32)
    decay = decay_row(in_ref[0])
    for i in range(1, OWNERS):
        d = decay_row(in_ref[i])
        state = state * d + in_ref[i, :STATE, :].astype(f32)
        decay = decay * d
    out_ref[:STATE, :] = state.astype(bf16)
    out_ref[STATE:, :] = pack_rows(decay)


def join_kernel(place_ref, own_ref, other_ref, pair_ref):
    second = place_ref[0] % 2 == 1
    own, other = own_ref[...].astype(f32), other_ref[...].astype(f32)
    late = jnp.where(second, own, other)
    early = jnp.where(second, other, own)
    late_decay, early_decay = decay_row(late), decay_row(early)
    pair_ref[:STATE, :] = (late[:STATE] + late_decay * early[:STATE]).astype(bf16)
    pair_ref[STATE:, :] = pack_rows(late_decay * early_decay)


def held_kernel(place_ref, other_ref, pair_ref, in_ref, out_hbm, out_buf, sem):
    place = place_ref[0]
    state = jnp.where(place >= 2, pair_ref[:STATE, :].astype(f32), 0.0)
    other = other_ref[...].astype(f32)
    state = jnp.where(place % 2 == 1, other[:STATE] + decay_row(other) * state, state)
    size = OWNERS // PIECES
    sent = []
    for i in range(OWNERS):
        out_buf[i] = state.astype(bf16)
        if (i + 1) % size == 0:
            span = pl.ds(i + 1 - size, size)
            sent += copies((out_buf.at[span], out_hbm.at[span], sem.at[i // size]))
        if i + 1 < OWNERS:
            state = state * decay_row(in_ref[i]) + in_ref[i, :STATE, :].astype(f32)
    for c in sent:
        c.wait()


def total_of(arrived):
    return pl.pallas_call(
        total_kernel,
        out_shape=jax.ShapeDtypeStruct((ROWS, COLS), bf16),
        compiler_params=pltpu.CompilerParams(vmem_limit_bytes=SMALL_VMEM_LIMIT),
        cost_estimate=pl.CostEstimate(flops=4_000_000, bytes_accessed=2_000_000, transcendentals=0),
        name="total",
    )(arrived)


def pair_of(place, own, other):
    vmem = pl.BlockSpec(memory_space=pltpu.VMEM)
    return pl.pallas_call(
        join_kernel,
        out_shape=jax.ShapeDtypeStruct((ROWS, COLS), bf16),
        in_specs=[pl.BlockSpec(memory_space=pltpu.SMEM), vmem, vmem],
        compiler_params=pltpu.CompilerParams(vmem_limit_bytes=SMALL_VMEM_LIMIT),
        cost_estimate=pl.CostEstimate(flops=100_000, bytes_accessed=100_000, transcendentals=0),
        name="pair",
    )(place, own, other)


def held_of(place, other, pair, arrived):
    vmem = pl.BlockSpec(memory_space=pltpu.VMEM)
    return pl.pallas_call(
        held_kernel,
        out_shape=pltpu.HBM((OWNERS, STATE, COLS), bf16),
        in_specs=[pl.BlockSpec(memory_space=pltpu.SMEM), vmem, vmem, vmem],
        out_specs=pl.BlockSpec(memory_space=pltpu.HBM),
        scratch_shapes=[
            pltpu.VMEM((OWNERS, STATE, COLS), bf16),
            pltpu.SemaphoreType.DMA((PIECES,)),
        ],
        compiler_params=pltpu.CompilerParams(vmem_limit_bytes=HELD_VMEM_LIMIT),
        cost_estimate=pl.CostEstimate(flops=4_000_000, bytes_accessed=4_000_000, transcendentals=0),
        name="held",
    )(place, other, pair, arrived)


def local_kernel(
    part, x_hbm, step_hbm, decay_hbm, inject_hbm, readout_hbm, gain_ref, *rest
):
    if part == 0:
        out_hbm, lead_ref = rest[:2]
    else:
        out_hbm = rest[1]
    x_buf, step_buf, decay_buf, inject_buf, readout_buf, out_buf, sem, in_sem, out_sem = rest[2:]
    decay_in, step_in, inject_in, readout_in = copies(
        (decay_hbm, decay_buf, sem.at[0]),
        (step_hbm, step_buf, sem.at[1]),
        (inject_hbm, inject_buf, sem.at[2]),
        (readout_hbm, readout_buf, sem.at[3]),
    )
    x_in = copies(
        *[
            (
                x_hbm.at[:, pl.ds(part * PART_COLS + n * GROUP_COLS, GROUP_COLS)],
                x_buf.at[n],
                in_sem.at[n],
            )
            for n in range(PART_GROUPS)
        ]
    )
    lower = iota((HALF, HALF), 0) >= iota((HALF, HALF), 1)
    lower_f = jnp.where(lower, 1.0, 0.0).astype(f32)
    decay_in.wait()
    cum_a = sums(lower_f, decay_buf[:HALF])
    cum_b = sums(lower_f, decay_buf[HALF:])
    if part == 0:
        lead_ref[:HALF] = jnp.exp(cum_a)
        lead_ref[HALF:] = jnp.exp(cum_b + cum_a[HALF - 1 : HALF])
    mid = HALF // 2 - 1
    mid_b = cum_b[mid : mid + 1]
    gap_a = cum_a - cum_a[mid : mid + 1]
    gap_b = cum_b - mid_b
    onward = jnp.exp(mid_b + gap_a[HALF - 1 : HALF])
    few = iota((8, HEADS), 0)
    rows = jnp.where(few == 0, onward, gain_ref[...])
    step_in.wait()
    into_a = step_buf[:HALF] * jnp.exp(-gap_a)
    into_b = step_buf[HALF:] * jnp.exp(-gap_b)
    from_a = jnp.exp(gap_a)
    from_b = jnp.exp(gap_b)
    zero = jnp.zeros((HALF, HALF), f32)
    inject_in.wait()
    readout_in.wait()

    def pair(r, i):
        return lax.dot_general(r, i, (((1,), (1,)), ((), ())), preferred_element_type=f32)

    sent = []
    for n in range(PART_GROUPS):
        g = part * PART_GROUPS + n
        state_cols = slice(g * STATE, (g + 1) * STATE)
        inj_a = inject_buf[:HALF, state_cols]
        inj_b = inject_buf[HALF:, state_cols]
        read_a = readout_buf[:HALF, state_cols]
        read_b = readout_buf[HALF:, state_cols]
        near_a = jnp.where(lower, pair(read_a, inj_a), zero).astype(bf16)
        near_b = jnp.concatenate(
            [
                pair(read_b, inj_a).astype(bf16),
                jnp.where(lower, pair(read_b, inj_b), zero).astype(bf16),
            ],
            axis=1,
        )
        x_in[n].wait()
        for k in range(GROUP_COLS // WIDE):
            cols = slice(k * WIDE, (k + 1) * WIDE)
            at = g * GROUP_COLS + k * WIDE
            row = spread(rows, at, WIDE)
            gain = row[1:2]
            x_a = x_buf[n, :HALF, cols].astype(f32)
            x_b = x_buf[n, HALF:, cols].astype(f32)
            v_a = x_a * spread(into_a, at, WIDE)
            v_b = (x_b * spread(into_b, at, WIDE)).astype(bf16)
            res_a = dot(near_a, v_a.astype(bf16))
            res_b = dot(near_b, jnp.concatenate([(v_a * row[0:1]).astype(bf16), v_b], axis=0))
            out_a = res_a * spread(from_a, at, WIDE) + gain * x_a
            out_b = res_b * spread(from_b, at, WIDE) + gain * x_b
            out_buf[n, :HALF, cols] = out_a.astype(bf16)
            out_buf[n, HALF:, cols] = out_b.astype(bf16)
        sent += copies(
            (out_buf.at[n], out_hbm.at[:, pl.ds(g * GROUP_COLS, GROUP_COLS)], out_sem.at[n])
        )
    for c in sent:
        c.wait()


def local_of(part, so_far, x, step, decay, inject, readout, gain):
    hbm = pl.BlockSpec(memory_space=pltpu.HBM)
    vmem = pl.BlockSpec(memory_space=pltpu.VMEM)
    return pl.pallas_call(
        functools.partial(local_kernel, part),
        out_shape=[jax.ShapeDtypeStruct(x.shape, bf16)]
        + ([] if so_far else [jax.ShapeDtypeStruct((TOK, HEADS), f32)]),
        in_specs=[hbm] * 5 + [vmem] + [hbm] * len(so_far),
        input_output_aliases={6: 0} if so_far else {},
        out_specs=[hbm] if so_far else [hbm, vmem],
        scratch_shapes=[
            pltpu.VMEM((PART_GROUPS, TOK, GROUP_COLS), bf16),
            pltpu.VMEM((TOK, HEADS), f32),
            pltpu.VMEM((TOK, HEADS), f32),
            pltpu.VMEM((TOK, GROUPS * STATE), bf16),
            pltpu.VMEM((TOK, GROUPS * STATE), bf16),
            pltpu.VMEM((PART_GROUPS, TOK, GROUP_COLS), bf16),
            pltpu.SemaphoreType.DMA((4,)),
            pltpu.SemaphoreType.DMA((PART_GROUPS,)),
            pltpu.SemaphoreType.DMA((PART_GROUPS,)),
        ],
        compiler_params=pltpu.CompilerParams(vmem_limit_bytes=VMEM_LIMIT),
        cost_estimate=pl.CostEstimate(
            flops=2_000_000_000, bytes_accessed=6_000_000, transcendentals=65536
        ),
        name=f"local{part}",
    )(x, step, decay, inject, readout, gain, *so_far)


def out_kernel(
    lead_ref, readout_ref, held_ref, local_hbm, out_hbm, far_buf, local_buf, out_buf, local_sem, out_sem
):
    local_in = copies(
        *[
            (local_hbm.at[:, pl.ds(g * GROUP_COLS, GROUP_COLS)], local_buf.at[g], local_sem.at[g])
            for g in range(GROUPS)
        ]
    )
    sent = []
    for g in range(GROUPS + 1):
        if g > 0:
            local_in[g - 1].wait()
        if g < GROUPS:
            held = jnp.concatenate(
                [held_ref[g * GROUP_OWNERS + i] for i in range(GROUP_OWNERS)], axis=1
            )
            far_buf[g % 2] = dot(readout_ref[:, g * STATE : (g + 1) * STATE], held)
        if g > 0:
            at = (g - 1) * GROUP_COLS
            far = far_buf[(g - 1) % 2] * spread(lead_ref[...], at, GROUP_COLS)
            out_buf[g - 1] = (far + local_buf[g - 1].astype(f32)).astype(bf16)
            sent += copies(
                (out_buf.at[g - 1], out_hbm.at[:, pl.ds(at, GROUP_COLS)], out_sem.at[g - 1])
            )
    for c in sent:
        c.wait()


def outputs_of(lead, readout, held, local):
    hbm = pl.BlockSpec(memory_space=pltpu.HBM)
    vmem = pl.BlockSpec(memory_space=pltpu.VMEM)
    return pl.pallas_call(
        out_kernel,
        out_shape=jax.ShapeDtypeStruct((TOK, HEADS * HEAD_DIM), bf16),
        in_specs=[vmem, vmem, vmem, hbm],
        out_specs=hbm,
        scratch_shapes=[
            pltpu.VMEM((2, TOK, GROUP_COLS), f32),
            pltpu.VMEM((GROUPS, TOK, GROUP_COLS), bf16),
            pltpu.VMEM((GROUPS, TOK, GROUP_COLS), bf16),
            pltpu.SemaphoreType.DMA((GROUPS,)),
            pltpu.SemaphoreType.DMA((GROUPS,)),
        ],
        compiler_params=pltpu.CompilerParams(vmem_limit_bytes=OUT_VMEM_LIMIT),
        cost_estimate=pl.CostEstimate(
            flops=2_000_000_000, bytes_accessed=12_000_000, transcendentals=0
        ),
        name="outputs",
    )(lead, readout, held, local)


def swap_runs(v, bit, ways):
    return lax.ppermute(v, "seq", [(i, i ^ (bit * STEP)) for i in range(ways)])


def exchange(v, devices):
    return lax.all_to_all(
        v,
        ("seq", "head"),
        split_axis=0,
        concat_axis=0,
        tiled=True,
        axis_index_groups=[
            list(range(first, first + OWNERS)) for first in range(0, devices, OWNERS)
        ],
    )


def shards(features, step_size, log_decay, inject, readout, skip_gain):
    ways = lax.axis_size("seq")
    devices = ways * lax.axis_size("head")
    args = (features, step_size, log_decay, inject, readout, skip_gain[None, :])
    arrived = exchange(states_of(features, step_size, log_decay, inject), devices)
    local, lead = local_of(0, (), *args)
    arrived, local, lead = lax.optimization_barrier((arrived, local, lead))
    place = (lax.axis_index("seq") // STEP).astype(jnp.int32)[None]
    total = total_of(arrived)
    other = swap_runs(total, 1, ways)
    pair = swap_runs(pair_of(place, total, other), 2, ways)
    held = held_of(place, other, pair, arrived)
    held = exchange(held, devices)
    (local,) = local_of(1, (local,), *args)
    return outputs_of(lead, readout, held, local)


def solution(mesh):
    rows = P(("seq", "head"), None)
    return jax.shard_map(
        shards,
        mesh=mesh,
        in_specs=(rows, rows, rows, rows, rows, P()),
        out_specs=rows,
        check_vma=False,
    )
```

```python
import functools

import jax
import jax.numpy as jnp
from jax import lax
from jax.experimental import pallas as pl
from jax.experimental.pallas import tpu as pltpu
from jax.sharding import PartitionSpec as P

HEADS = 128
HEAD_DIM = 64
STATE = 128
GROUPS = 8
TOK = 256
HALF = 128
LANES = 128
OWNERS = 64
STEP = 4
PIECES = 4
OWN_HEADS = HEADS // OWNERS
COLS = OWN_HEADS * HEAD_DIM
GROUP_COLS = HEADS // GROUPS * HEAD_DIM
GROUP_OWNERS = OWNERS // GROUPS
ROWS = STATE + 8
VMEM_LIMIT = 61 * 1024 * 1024
OUT_VMEM_LIMIT = 50 * 1024 * 1024
HELD_VMEM_LIMIT = 40 * 1024 * 1024
SMALL_VMEM_LIMIT = 24 * 1024 * 1024
WIDE = 512
NARROW = 256
LOCAL_PARTS = 2
PART_GROUPS = GROUPS // LOCAL_PARTS
PART_COLS = PART_GROUPS * GROUP_COLS

f32 = jnp.float32
bf16 = jnp.bfloat16


def dot(a, b):
    return jnp.dot(a, b, preferred_element_type=f32)


def sums(mask, v):
    high = v.astype(bf16)
    rest = v - high.astype(f32)
    middle = rest.astype(bf16)
    low = (rest - middle.astype(f32)).astype(bf16)
    p = dot(mask.astype(bf16), jnp.concatenate([high, middle, low], axis=1))
    return p[:, :HEADS] + p[:, HEADS : 2 * HEADS] + p[:, 2 * HEADS :]


def iota(shape, axis):
    return lax.broadcasted_iota(jnp.int32, shape, axis)


def spread(scale, first_col, cols):
    place = iota((scale.shape[0], LANES), 1) >> 6
    first_head = first_col // HEAD_DIM
    return jnp.concatenate(
        [
            jnp.take_along_axis(
                scale, place + (first_head + 2 * k), axis=1, mode="promise_in_bounds"
            )
            for k in range(cols // LANES)
        ],
        axis=1,
    )


def copies(*triples):
    made = [pltpu.make_async_copy(*t) for t in triples]
    for c in made:
        c.start()
    return made


def state_kernel(
    x_hbm, step_hbm, decay_hbm, inject_hbm, out_hbm,
    x_buf, step_buf, decay_buf, inject_buf, turned_buf, v_buf, out_buf, sem, in_sem, out_sem,
):
    decay_in, step_in, inject_in = copies(
        (decay_hbm, decay_buf, sem.at[0]),
        (step_hbm, step_buf, sem.at[1]),
        (inject_hbm, inject_buf, sem.at[2]),
    )
    x_in = copies(
        *[
            (x_hbm.at[:, pl.ds(g * GROUP_COLS, GROUP_COLS)], x_buf.at[g], in_sem.at[g])
            for g in range(GROUPS)
        ]
    )
    later = jnp.where(iota((TOK, TOK), 1) > iota((TOK, TOK), 0), 1.0, 0.0).astype(f32)
    decay_in.wait()
    decay = decay_buf[...]
    tail = sums(later, decay)
    whole = jnp.broadcast_to(jnp.exp(tail[0:1] + decay[0:1]), (8, HEADS))
    high = whole.astype(bf16).astype(f32)
    row = iota((8, HEADS), 0)
    extra = jnp.where(row == 0, high, jnp.where(row == 1, whole - high, 0.0))
    step_in.wait()
    scale = step_buf[...] * jnp.exp(tail)
    inject_in.wait()
    for g in range(GROUPS):
        turned_buf[g] = inject_buf[:, g * STATE : (g + 1) * STATE].T
    sent = []
    for g in range(GROUPS + 1):
        if g < GROUPS:
            if g % 4 == 0:
                for c in x_in[g : g + 4]:
                    c.wait()
        first = (g - 1) * GROUP_OWNERS
        for w in range(GROUP_COLS // NARROW):
            part = slice(w * NARROW, (w + 1) * NARROW)
            if g < GROUPS:
                weight = spread(scale, g * GROUP_COLS + w * NARROW, NARROW)
                v_buf[g % 2, :, part] = x_buf[g, :, part] * weight.astype(bf16)
            if g > 0:
                s = dot(turned_buf[g - 1], v_buf[(g - 1) % 2, :, part]).astype(bf16)
                below = spread(extra, (g - 1) * GROUP_COLS + w * NARROW, NARROW).astype(bf16)
                for k in range(NARROW // COLS):
                    cols = slice(k * COLS, (k + 1) * COLS)
                    owner = first + w * (NARROW // COLS) + k
                    out_buf[owner, :STATE, :] = s[:, cols]
                    out_buf[owner, STATE:, :] = below[:, cols]
        if g > 0:
            span = pl.ds(first, GROUP_OWNERS)
            sent += copies((out_buf.at[span], out_hbm.at[span], out_sem.at[g - 1]))
    for c in sent:
        c.wait()


def states_of(x, step, decay, inject):
    hbm = pl.BlockSpec(memory_space=pltpu.HBM)
    return pl.pallas_call(
        state_kernel,
        out_shape=jax.ShapeDtypeStruct((OWNERS, ROWS, COLS), bf16),
        in_specs=[hbm] * 4,
        out_specs=hbm,
        scratch_shapes=[
            pltpu.VMEM((GROUPS, TOK, GROUP_COLS), bf16),
            pltpu.VMEM((TOK, HEADS), f32),
            pltpu.VMEM((TOK, HEADS), f32),
            pltpu.VMEM((TOK, GROUPS * STATE), bf16),
            pltpu.VMEM((GROUPS, STATE, TOK), bf16),
            pltpu.VMEM((2, TOK, GROUP_COLS), bf16),
            pltpu.VMEM((OWNERS, ROWS, COLS), bf16),
            pltpu.SemaphoreType.DMA((3,)),
            pltpu.SemaphoreType.DMA((GROUPS,)),
            pltpu.SemaphoreType.DMA((GROUPS,)),
        ],
        compiler_params=pltpu.CompilerParams(vmem_limit_bytes=VMEM_LIMIT),
        cost_estimate=pl.CostEstimate(
            flops=2_000_000_000, bytes_accessed=8_000_000, transcendentals=32768
        ),
        name="states",
    )(x, step, decay, inject)


def decay_row(block):
    return block[STATE : STATE + 1].astype(f32) + block[STATE + 1 : STATE + 2].astype(f32)


def pack_rows(decay):
    row = iota((8, COLS), 0)
    high = decay.astype(bf16).astype(f32)
    return jnp.where(row == 0, high, jnp.where(row == 1, decay - high, 0.0)).astype(bf16)


def total_kernel(in_ref, out_ref):
    state = in_ref[0, :STATE, :].astype(f32)
    decay = decay_row(in_ref[0])
    for i in range(1, OWNERS):
        d = decay_row(in_ref[i])
        state = state * d + in_ref[i, :STATE, :].astype(f32)
        decay = decay * d
    out_ref[:STATE, :] = state.astype(bf16)
    out_ref[STATE:, :] = pack_rows(decay)


def join_kernel(place_ref, own_ref, other_ref, pair_ref):
    second = place_ref[0] % 2 == 1
    own, other = own_ref[...].astype(f32), other_ref[...].astype(f32)
    late = jnp.where(second, own, other)
    early = jnp.where(second, other, own)
    late_decay, early_decay = decay_row(late), decay_row(early)
    pair_ref[:STATE, :] = (late[:STATE] + late_decay * early[:STATE]).astype(bf16)
    pair_ref[STATE:, :] = pack_rows(late_decay * early_decay)


def held_kernel(place_ref, other_ref, pair_ref, in_ref, out_hbm, out_buf, sem):
    place = place_ref[0]
    state = jnp.where(place >= 2, pair_ref[:STATE, :].astype(f32), 0.0)
    other = other_ref[...].astype(f32)
    state = jnp.where(place % 2 == 1, other[:STATE] + decay_row(other) * state, state)
    size = OWNERS // PIECES
    sent = []
    for i in range(OWNERS):
        out_buf[i] = state.astype(bf16)
        if (i + 1) % size == 0:
            span = pl.ds(i + 1 - size, size)
            sent += copies((out_buf.at[span], out_hbm.at[span], sem.at[i // size]))
        if i + 1 < OWNERS:
            state = state * decay_row(in_ref[i]) + in_ref[i, :STATE, :].astype(f32)
    for c in sent:
        c.wait()


def total_of(arrived):
    return pl.pallas_call(
        total_kernel,
        out_shape=jax.ShapeDtypeStruct((ROWS, COLS), bf16),
        compiler_params=pltpu.CompilerParams(vmem_limit_bytes=SMALL_VMEM_LIMIT),
        cost_estimate=pl.CostEstimate(flops=4_000_000, bytes_accessed=2_000_000, transcendentals=0),
        name="total",
    )(arrived)


def pair_of(place, own, other):
    vmem = pl.BlockSpec(memory_space=pltpu.VMEM)
    return pl.pallas_call(
        join_kernel,
        out_shape=jax.ShapeDtypeStruct((ROWS, COLS), bf16),
        in_specs=[pl.BlockSpec(memory_space=pltpu.SMEM), vmem, vmem],
        compiler_params=pltpu.CompilerParams(vmem_limit_bytes=SMALL_VMEM_LIMIT),
        cost_estimate=pl.CostEstimate(flops=100_000, bytes_accessed=100_000, transcendentals=0),
        name="pair",
    )(place, own, other)


def held_of(place, other, pair, arrived):
    vmem = pl.BlockSpec(memory_space=pltpu.VMEM)
    return pl.pallas_call(
        held_kernel,
        out_shape=pltpu.HBM((OWNERS, STATE, COLS), bf16),
        in_specs=[pl.BlockSpec(memory_space=pltpu.SMEM), vmem, vmem, vmem],
        out_specs=pl.BlockSpec(memory_space=pltpu.HBM),
        scratch_shapes=[
            pltpu.VMEM((OWNERS, STATE, COLS), bf16),
            pltpu.SemaphoreType.DMA((PIECES,)),
        ],
        compiler_params=pltpu.CompilerParams(vmem_limit_bytes=HELD_VMEM_LIMIT),
        cost_estimate=pl.CostEstimate(flops=4_000_000, bytes_accessed=4_000_000, transcendentals=0),
        name="held",
    )(place, other, pair, arrived)


def local_kernel(
    part, x_hbm, step_hbm, decay_hbm, inject_hbm, readout_hbm, gain_ref, *rest
):
    if part == 0:
        out_hbm, lead_ref = rest[:2]
    else:
        out_hbm = rest[1]
    x_buf, step_buf, decay_buf, inject_buf, readout_buf, out_buf, sem, in_sem, out_sem = rest[2:]
    decay_in, step_in, inject_in, readout_in = copies(
        (decay_hbm, decay_buf, sem.at[0]),
        (step_hbm, step_buf, sem.at[1]),
        (inject_hbm, inject_buf, sem.at[2]),
        (readout_hbm, readout_buf, sem.at[3]),
    )
    x_in = copies(
        *[
            (
                x_hbm.at[:, pl.ds(part * PART_COLS + n * GROUP_COLS, GROUP_COLS)],
                x_buf.at[n],
                in_sem.at[n],
            )
            for n in range(PART_GROUPS)
        ]
    )
    lower = iota((HALF, HALF), 0) >= iota((HALF, HALF), 1)
    lower_f = jnp.where(lower, 1.0, 0.0).astype(f32)
    decay_in.wait()
    cum_a = sums(lower_f, decay_buf[:HALF])
    cum_b = sums(lower_f, decay_buf[HALF:])
    if part == 0:
        lead_ref[:HALF] = jnp.exp(cum_a)
        lead_ref[HALF:] = jnp.exp(cum_b + cum_a[HALF - 1 : HALF])
    mid = HALF // 2 - 1
    mid_b = cum_b[mid : mid + 1]
    gap_a = cum_a - cum_a[mid : mid + 1]
    gap_b = cum_b - mid_b
    onward = jnp.exp(mid_b + gap_a[HALF - 1 : HALF])
    few = iota((8, HEADS), 0)
    rows = jnp.where(few == 0, onward, gain_ref[...])
    step_in.wait()
    into_a = step_buf[:HALF] * jnp.exp(-gap_a)
    into_b = step_buf[HALF:] * jnp.exp(-gap_b)
    from_a = jnp.exp(gap_a)
    from_b = jnp.exp(gap_b)
    zero = jnp.zeros((HALF, HALF), f32)
    inject_in.wait()
    readout_in.wait()

    def pair(r, i):
        return lax.dot_general(r, i, (((1,), (1,)), ((), ())), preferred_element_type=f32)

    sent = []
    for n in range(PART_GROUPS):
        g = part * PART_GROUPS + n
        state_cols = slice(g * STATE, (g + 1) * STATE)
        inj_a = inject_buf[:HALF, state_cols]
        inj_b = inject_buf[HALF:, state_cols]
        read_a = readout_buf[:HALF, state_cols]
        read_b = readout_buf[HALF:, state_cols]
        near_a = jnp.where(lower, pair(read_a, inj_a), zero).astype(bf16)
        near_b = jnp.concatenate(
            [
                pair(read_b, inj_a).astype(bf16),
                jnp.where(lower, pair(read_b, inj_b), zero).astype(bf16),
            ],
            axis=1,
        )
        x_in[n].wait()
        for k in range(GROUP_COLS // WIDE):
            cols = slice(k * WIDE, (k + 1) * WIDE)
            at = g * GROUP_COLS + k * WIDE
            row = spread(rows, at, WIDE)
            gain = row[1:2]
            x_a = x_buf[n, :HALF, cols].astype(f32)
            x_b = x_buf[n, HALF:, cols].astype(f32)
            v_a = x_a * spread(into_a, at, WIDE)
            v_b = (x_b * spread(into_b, at, WIDE)).astype(bf16)
            res_a = dot(near_a, v_a.astype(bf16))
            res_b = dot(near_b, jnp.concatenate([(v_a * row[0:1]).astype(bf16), v_b], axis=0))
            out_a = res_a * spread(from_a, at, WIDE) + gain * x_a
            out_b = res_b * spread(from_b, at, WIDE) + gain * x_b
            out_buf[n, :HALF, cols] = out_a.astype(bf16)
            out_buf[n, HALF:, cols] = out_b.astype(bf16)
        sent += copies(
            (out_buf.at[n], out_hbm.at[:, pl.ds(g * GROUP_COLS, GROUP_COLS)], out_sem.at[n])
        )
    for c in sent:
        c.wait()


def local_of(part, so_far, x, step, decay, inject, readout, gain):
    hbm = pl.BlockSpec(memory_space=pltpu.HBM)
    vmem = pl.BlockSpec(memory_space=pltpu.VMEM)
    return pl.pallas_call(
        functools.partial(local_kernel, part),
        out_shape=[jax.ShapeDtypeStruct(x.shape, bf16)]
        + ([] if so_far else [jax.ShapeDtypeStruct((TOK, HEADS), f32)]),
        in_specs=[hbm] * 5 + [vmem] + [hbm] * len(so_far),
        input_output_aliases={6: 0} if so_far else {},
        out_specs=[hbm] if so_far else [hbm, vmem],
        scratch_shapes=[
            pltpu.VMEM((PART_GROUPS, TOK, GROUP_COLS), bf16),
            pltpu.VMEM((TOK, HEADS), f32),
            pltpu.VMEM((TOK, HEADS), f32),
            pltpu.VMEM((TOK, GROUPS * STATE), bf16),
            pltpu.VMEM((TOK, GROUPS * STATE), bf16),
            pltpu.VMEM((PART_GROUPS, TOK, GROUP_COLS), bf16),
            pltpu.SemaphoreType.DMA((4,)),
            pltpu.SemaphoreType.DMA((PART_GROUPS,)),
            pltpu.SemaphoreType.DMA((PART_GROUPS,)),
        ],
        compiler_params=pltpu.CompilerParams(vmem_limit_bytes=VMEM_LIMIT),
        cost_estimate=pl.CostEstimate(
            flops=2_000_000_000, bytes_accessed=6_000_000, transcendentals=65536
        ),
        name=f"local{part}",
    )(x, step, decay, inject, readout, gain, *so_far)


def out_kernel(
    lead_ref, readout_ref, held_ref, local_hbm, out_hbm, far_buf, local_buf, out_buf, local_sem, out_sem
):
    local_in = copies(
        *[
            (local_hbm.at[:, pl.ds(g * GROUP_COLS, GROUP_COLS)], local_buf.at[g], local_sem.at[g])
            for g in range(GROUPS)
        ]
    )
    sent = []
    for g in range(GROUPS + 1):
        if g % 2 == 1:
            local_in[g - 1].wait()
            local_in[g].wait()
        if g < GROUPS:
            held = jnp.concatenate(
                [held_ref[g * GROUP_OWNERS + i] for i in range(GROUP_OWNERS)], axis=1
            )
            far_buf[g % 2] = dot(readout_ref[:, g * STATE : (g + 1) * STATE], held)
        if g > 0:
            at = (g - 1) * GROUP_COLS
            far = far_buf[(g - 1) % 2] * spread(lead_ref[...], at, GROUP_COLS)
            out_buf[g - 1] = (far + local_buf[g - 1].astype(f32)).astype(bf16)
            sent += copies(
                (out_buf.at[g - 1], out_hbm.at[:, pl.ds(at, GROUP_COLS)], out_sem.at[g - 1])
            )
    for c in sent:
        c.wait()


def outputs_of(lead, readout, held, local):
    hbm = pl.BlockSpec(memory_space=pltpu.HBM)
    vmem = pl.BlockSpec(memory_space=pltpu.VMEM)
    return pl.pallas_call(
        out_kernel,
        out_shape=jax.ShapeDtypeStruct((TOK, HEADS * HEAD_DIM), bf16),
        in_specs=[vmem, vmem, vmem, hbm],
        out_specs=hbm,
        scratch_shapes=[
            pltpu.VMEM((2, TOK, GROUP_COLS), f32),
            pltpu.VMEM((GROUPS, TOK, GROUP_COLS), bf16),
            pltpu.VMEM((GROUPS, TOK, GROUP_COLS), bf16),
            pltpu.SemaphoreType.DMA((GROUPS,)),
            pltpu.SemaphoreType.DMA((GROUPS,)),
        ],
        compiler_params=pltpu.CompilerParams(vmem_limit_bytes=OUT_VMEM_LIMIT),
        cost_estimate=pl.CostEstimate(
            flops=2_000_000_000, bytes_accessed=12_000_000, transcendentals=0
        ),
        name="outputs",
    )(lead, readout, held, local)


def swap_runs(v, bits, ways):
    return lax.ppermute(v, "seq", [(i, i ^ (bits * STEP)) for i in range(ways)])


def exchange(v, devices):
    return lax.all_to_all(
        v,
        ("seq", "head"),
        split_axis=0,
        concat_axis=0,
        tiled=True,
        axis_index_groups=[
            list(range(first, first + OWNERS)) for first in range(0, devices, OWNERS)
        ],
    )


def shards(features, step_size, log_decay, inject, readout, skip_gain):
    ways = lax.axis_size("seq")
    devices = ways * lax.axis_size("head")
    args = (features, step_size, log_decay, inject, readout, skip_gain[None, :])
    arrived = exchange(states_of(features, step_size, log_decay, inject), devices)
    local, lead = local_of(0, (), *args)
    arrived, local, lead = lax.optimization_barrier((arrived, local, lead))
    place = (lax.axis_index("seq") // STEP).astype(jnp.int32)[None]
    total = total_of(arrived)
    other = swap_runs(total, 1, ways)
    pair = swap_runs(pair_of(place, total, other), 3, ways)
    held = held_of(place, other, pair, arrived)
    held = exchange(held, devices)
    (local,) = local_of(1, (local,), *args)
    return outputs_of(lead, readout, held, local)


def solution(mesh):
    rows = P(("seq", "head"), None)
    return jax.shard_map(
        shards,
        mesh=mesh,
        in_specs=(rows, rows, rows, rows, rows, P()),
        out_specs=rows,
        check_vma=False,
    )
```

```python
import functools

import jax
import jax.numpy as jnp
from jax import lax
from jax.experimental import pallas as pl
from jax.experimental.pallas import tpu as pltpu
from jax.sharding import PartitionSpec as P

HEADS = 128
HEAD_DIM = 64
STATE = 128
GROUPS = 8
TOK = 256
HALF = 128
LANES = 128
OWNERS = 64
STEP = 4
PIECES = 4
OWN_HEADS = HEADS // OWNERS
COLS = OWN_HEADS * HEAD_DIM
GROUP_COLS = HEADS // GROUPS * HEAD_DIM
GROUP_OWNERS = OWNERS // GROUPS
ROWS = STATE + 8
VMEM_LIMIT = 61 * 1024 * 1024
OUT_VMEM_LIMIT = 50 * 1024 * 1024
HELD_VMEM_LIMIT = 40 * 1024 * 1024
SMALL_VMEM_LIMIT = 24 * 1024 * 1024
WIDE = 512
NARROW = 256
LOCAL_PARTS = 2
PART_GROUPS = GROUPS // LOCAL_PARTS
PART_COLS = PART_GROUPS * GROUP_COLS

f32 = jnp.float32
bf16 = jnp.bfloat16


def dot(a, b):
    return jnp.dot(a, b, preferred_element_type=f32)


def sums(mask, v):
    high = v.astype(bf16)
    rest = v - high.astype(f32)
    middle = rest.astype(bf16)
    low = (rest - middle.astype(f32)).astype(bf16)
    p = dot(mask.astype(bf16), jnp.concatenate([high, middle, low], axis=1))
    return p[:, :HEADS] + p[:, HEADS : 2 * HEADS] + p[:, 2 * HEADS :]


def iota(shape, axis):
    return lax.broadcasted_iota(jnp.int32, shape, axis)


def spread(scale, first_col, cols):
    place = iota((scale.shape[0], LANES), 1) >> 6
    first_head = first_col // HEAD_DIM
    return jnp.concatenate(
        [
            jnp.take_along_axis(
                scale, place + (first_head + 2 * k), axis=1, mode="promise_in_bounds"
            )
            for k in range(cols // LANES)
        ],
        axis=1,
    )


def copies(*triples):
    made = [pltpu.make_async_copy(*t) for t in triples]
    for c in made:
        c.start()
    return made


def state_kernel(
    x_hbm, step_hbm, decay_hbm, inject_hbm, out_hbm,
    x_buf, step_buf, decay_buf, inject_buf, turned_buf, v_buf, out_buf, sem, in_sem, out_sem,
):
    decay_in, step_in, inject_in = copies(
        (decay_hbm, decay_buf, sem.at[0]),
        (step_hbm, step_buf, sem.at[1]),
        (inject_hbm, inject_buf, sem.at[2]),
    )
    x_in = copies(
        *[
            (x_hbm.at[:, pl.ds(g * GROUP_COLS, GROUP_COLS)], x_buf.at[g], in_sem.at[g])
            for g in range(GROUPS)
        ]
    )
    later = jnp.where(iota((TOK, TOK), 1) > iota((TOK, TOK), 0), 1.0, 0.0).astype(f32)
    decay_in.wait()
    decay = decay_buf[...]
    tail = sums(later, decay)
    whole = jnp.broadcast_to(jnp.exp(tail[0:1] + decay[0:1]), (8, HEADS))
    high = whole.astype(bf16).astype(f32)
    row = iota((8, HEADS), 0)
    extra = jnp.where(row == 0, high, jnp.where(row == 1, whole - high, 0.0))
    step_in.wait()
    scale = step_buf[...] * jnp.exp(tail)
    inject_in.wait()
    for g in range(GROUPS):
        turned_buf[g] = inject_buf[:, g * STATE : (g + 1) * STATE].T
    sent = []
    for g in range(GROUPS + 1):
        if g < GROUPS:
            if g % 4 == 0:
                for c in x_in[g : g + 4]:
                    c.wait()
        first = (g - 1) * GROUP_OWNERS
        for w in range(GROUP_COLS // NARROW):
            part = slice(w * NARROW, (w + 1) * NARROW)
            if g < GROUPS:
                weight = spread(scale, g * GROUP_COLS + w * NARROW, NARROW)
                v_buf[g % 2, :, part] = x_buf[g, :, part] * weight.astype(bf16)
            if g > 0:
                s = dot(turned_buf[g - 1], v_buf[(g - 1) % 2, :, part]).astype(bf16)
                below = spread(extra, (g - 1) * GROUP_COLS + w * NARROW, NARROW).astype(bf16)
                for k in range(NARROW // COLS):
                    cols = slice(k * COLS, (k + 1) * COLS)
                    owner = first + w * (NARROW // COLS) + k
                    out_buf[owner, :STATE, :] = s[:, cols]
                    out_buf[owner, STATE:, :] = below[:, cols]
        if g > 0:
            span = pl.ds(first, GROUP_OWNERS)
            sent += copies((out_buf.at[span], out_hbm.at[span], out_sem.at[g - 1]))
    for c in sent:
        c.wait()


def states_of(x, step, decay, inject):
    hbm = pl.BlockSpec(memory_space=pltpu.HBM)
    return pl.pallas_call(
        state_kernel,
        out_shape=jax.ShapeDtypeStruct((OWNERS, ROWS, COLS), bf16),
        in_specs=[hbm] * 4,
        out_specs=hbm,
        scratch_shapes=[
            pltpu.VMEM((GROUPS, TOK, GROUP_COLS), bf16),
            pltpu.VMEM((TOK, HEADS), f32),
            pltpu.VMEM((TOK, HEADS), f32),
            pltpu.VMEM((TOK, GROUPS * STATE), bf16),
            pltpu.VMEM((GROUPS, STATE, TOK), bf16),
            pltpu.VMEM((2, TOK, GROUP_COLS), bf16),
            pltpu.VMEM((OWNERS, ROWS, COLS), bf16),
            pltpu.SemaphoreType.DMA((3,)),
            pltpu.SemaphoreType.DMA((GROUPS,)),
            pltpu.SemaphoreType.DMA((GROUPS,)),
        ],
        compiler_params=pltpu.CompilerParams(vmem_limit_bytes=VMEM_LIMIT),
        cost_estimate=pl.CostEstimate(
            flops=2_000_000_000, bytes_accessed=8_000_000, transcendentals=32768
        ),
        name="states",
    )(x, step, decay, inject)


def decay_row(block):
    return block[STATE : STATE + 1].astype(f32) + block[STATE + 1 : STATE + 2].astype(f32)


def pack_rows(decay):
    row = iota((8, COLS), 0)
    high = decay.astype(bf16).astype(f32)
    return jnp.where(row == 0, high, jnp.where(row == 1, decay - high, 0.0)).astype(bf16)


def total_kernel(in_ref, out_ref):
    state = in_ref[0, :STATE, :].astype(f32)
    decay = decay_row(in_ref[0])
    for i in range(1, OWNERS):
        d = decay_row(in_ref[i])
        state = state * d + in_ref[i, :STATE, :].astype(f32)
        decay = decay * d
    out_ref[:STATE, :] = state.astype(bf16)
    out_ref[STATE:, :] = pack_rows(decay)


def held_kernel(place_ref, one_ref, two_ref, three_ref, in_ref, out_hbm, out_buf, sem):
    place = place_ref[0]
    state = jnp.zeros((STATE, COLS), f32)
    for run in range(3):
        bits = place ^ run
        block = jnp.where(
            bits == 1,
            one_ref[...].astype(f32),
            jnp.where(bits == 2, two_ref[...].astype(f32), three_ref[...].astype(f32)),
        )
        state = jnp.where(run < place, block[:STATE] + decay_row(block) * state, state)
    size = OWNERS // PIECES
    sent = []
    for i in range(OWNERS):
        out_buf[i] = state.astype(bf16)
        if (i + 1) % size == 0:
            span = pl.ds(i + 1 - size, size)
            sent += copies((out_buf.at[span], out_hbm.at[span], sem.at[i // size]))
        if i + 1 < OWNERS:
            state = state * decay_row(in_ref[i]) + in_ref[i, :STATE, :].astype(f32)
    for c in sent:
        c.wait()


def total_of(arrived):
    return pl.pallas_call(
        total_kernel,
        out_shape=jax.ShapeDtypeStruct((ROWS, COLS), bf16),
        compiler_params=pltpu.CompilerParams(vmem_limit_bytes=SMALL_VMEM_LIMIT),
        cost_estimate=pl.CostEstimate(flops=4_000_000, bytes_accessed=2_000_000, transcendentals=0),
        name="total",
    )(arrived)


def held_of(place, others, arrived):
    vmem = pl.BlockSpec(memory_space=pltpu.VMEM)
    return pl.pallas_call(
        held_kernel,
        out_shape=pltpu.HBM((OWNERS, STATE, COLS), bf16),
        in_specs=[pl.BlockSpec(memory_space=pltpu.SMEM)] + [vmem] * 4,
        out_specs=pl.BlockSpec(memory_space=pltpu.HBM),
        scratch_shapes=[
            pltpu.VMEM((OWNERS, STATE, COLS), bf16),
            pltpu.SemaphoreType.DMA((PIECES,)),
        ],
        compiler_params=pltpu.CompilerParams(vmem_limit_bytes=HELD_VMEM_LIMIT),
        cost_estimate=pl.CostEstimate(flops=4_000_000, bytes_accessed=4_000_000, transcendentals=0),
        name="held",
    )(place, *others, arrived)


def local_kernel(
    part, x_hbm, step_hbm, decay_hbm, inject_hbm, readout_hbm, gain_ref, *rest
):
    if part == 0:
        out_hbm, lead_ref = rest[:2]
    else:
        out_hbm = rest[1]
    x_buf, step_buf, decay_buf, inject_buf, readout_buf, out_buf, sem, in_sem, out_sem = rest[2:]
    decay_in, step_in, inject_in, readout_in = copies(
        (decay_hbm, decay_buf, sem.at[0]),
        (step_hbm, step_buf, sem.at[1]),
        (inject_hbm, inject_buf, sem.at[2]),
        (readout_hbm, readout_buf, sem.at[3]),
    )
    x_in = copies(
        *[
            (
                x_hbm.at[:, pl.ds(part * PART_COLS + n * GROUP_COLS, GROUP_COLS)],
                x_buf.at[n],
                in_sem.at[n],
            )
            for n in range(PART_GROUPS)
        ]
    )
    lower = iota((HALF, HALF), 0) >= iota((HALF, HALF), 1)
    lower_f = jnp.where(lower, 1.0, 0.0).astype(f32)
    decay_in.wait()
    cum_a = sums(lower_f, decay_buf[:HALF])
    cum_b = sums(lower_f, decay_buf[HALF:])
    if part == 0:
        lead_ref[:HALF] = jnp.exp(cum_a)
        lead_ref[HALF:] = jnp.exp(cum_b + cum_a[HALF - 1 : HALF])
    mid = HALF // 2 - 1
    mid_b = cum_b[mid : mid + 1]
    gap_a = cum_a - cum_a[mid : mid + 1]
    gap_b = cum_b - mid_b
    onward = jnp.exp(mid_b + gap_a[HALF - 1 : HALF])
    few = iota((8, HEADS), 0)
    rows = jnp.where(few == 0, onward, gain_ref[...])
    step_in.wait()
    into_a = step_buf[:HALF] * jnp.exp(-gap_a)
    into_b = step_buf[HALF:] * jnp.exp(-gap_b)
    from_a = jnp.exp(gap_a)
    from_b = jnp.exp(gap_b)
    zero = jnp.zeros((HALF, HALF), f32)
    inject_in.wait()
    readout_in.wait()

    def pair(r, i):
        return lax.dot_general(r, i, (((1,), (1,)), ((), ())), preferred_element_type=f32)

    sent = []
    for n in range(PART_GROUPS):
        g = part * PART_GROUPS + n
        state_cols = slice(g * STATE, (g + 1) * STATE)
        inj_a = inject_buf[:HALF, state_cols]
        inj_b = inject_buf[HALF:, state_cols]
        read_a = readout_buf[:HALF, state_cols]
        read_b = readout_buf[HALF:, state_cols]
        near_a = jnp.where(lower, pair(read_a, inj_a), zero).astype(bf16)
        near_b = jnp.concatenate(
            [
                pair(read_b, inj_a).astype(bf16),
                jnp.where(lower, pair(read_b, inj_b), zero).astype(bf16),
            ],
            axis=1,
        )
        x_in[n].wait()
        for k in range(GROUP_COLS // WIDE):
            cols = slice(k * WIDE, (k + 1) * WIDE)
            at = g * GROUP_COLS + k * WIDE
            row = spread(rows, at, WIDE)
            gain = row[1:2]
            x_a = x_buf[n, :HALF, cols].astype(f32)
            x_b = x_buf[n, HALF:, cols].astype(f32)
            v_a = x_a * spread(into_a, at, WIDE)
            v_b = (x_b * spread(into_b, at, WIDE)).astype(bf16)
            res_a = dot(near_a, v_a.astype(bf16))
            res_b = dot(near_b, jnp.concatenate([(v_a * row[0:1]).astype(bf16), v_b], axis=0))
            out_a = res_a * spread(from_a, at, WIDE) + gain * x_a
            out_b = res_b * spread(from_b, at, WIDE) + gain * x_b
            out_buf[n, :HALF, cols] = out_a.astype(bf16)
            out_buf[n, HALF:, cols] = out_b.astype(bf16)
        sent += copies(
            (out_buf.at[n], out_hbm.at[:, pl.ds(g * GROUP_COLS, GROUP_COLS)], out_sem.at[n])
        )
    for c in sent:
        c.wait()


def local_of(part, so_far, x, step, decay, inject, readout, gain):
    hbm = pl.BlockSpec(memory_space=pltpu.HBM)
    vmem = pl.BlockSpec(memory_space=pltpu.VMEM)
    return pl.pallas_call(
        functools.partial(local_kernel, part),
        out_shape=[jax.ShapeDtypeStruct(x.shape, bf16)]
        + ([] if so_far else [jax.ShapeDtypeStruct((TOK, HEADS), f32)]),
        in_specs=[hbm] * 5 + [vmem] + [hbm] * len(so_far),
        input_output_aliases={6: 0} if so_far else {},
        out_specs=[hbm] if so_far else [hbm, vmem],
        scratch_shapes=[
            pltpu.VMEM((PART_GROUPS, TOK, GROUP_COLS), bf16),
            pltpu.VMEM((TOK, HEADS), f32),
            pltpu.VMEM((TOK, HEADS), f32),
            pltpu.VMEM((TOK, GROUPS * STATE), bf16),
            pltpu.VMEM((TOK, GROUPS * STATE), bf16),
            pltpu.VMEM((PART_GROUPS, TOK, GROUP_COLS), bf16),
            pltpu.SemaphoreType.DMA((4,)),
            pltpu.SemaphoreType.DMA((PART_GROUPS,)),
            pltpu.SemaphoreType.DMA((PART_GROUPS,)),
        ],
        compiler_params=pltpu.CompilerParams(vmem_limit_bytes=VMEM_LIMIT),
        cost_estimate=pl.CostEstimate(
            flops=2_000_000_000, bytes_accessed=6_000_000, transcendentals=65536
        ),
        name=f"local{part}",
    )(x, step, decay, inject, readout, gain, *so_far)


def out_kernel(
    lead_ref, readout_ref, held_ref, local_hbm, out_hbm, far_buf, local_buf, out_buf, local_sem, out_sem
):
    local_in = copies(
        *[
            (local_hbm.at[:, pl.ds(g * GROUP_COLS, GROUP_COLS)], local_buf.at[g], local_sem.at[g])
            for g in range(GROUPS)
        ]
    )
    sent = []
    for g in range(GROUPS + 1):
        if g % 2 == 1:
            local_in[g - 1].wait()
            local_in[g].wait()
        if g < GROUPS:
            held = jnp.concatenate(
                [held_ref[g * GROUP_OWNERS + i] for i in range(GROUP_OWNERS)], axis=1
            )
            far_buf[g % 2] = dot(readout_ref[:, g * STATE : (g + 1) * STATE], held)
        if g > 0:
            at = (g - 1) * GROUP_COLS
            far = far_buf[(g - 1) % 2] * spread(lead_ref[...], at, GROUP_COLS)
            out_buf[g - 1] = (far + local_buf[g - 1].astype(f32)).astype(bf16)
            sent += copies(
                (out_buf.at[g - 1], out_hbm.at[:, pl.ds(at, GROUP_COLS)], out_sem.at[g - 1])
            )
    for c in sent:
        c.wait()


def outputs_of(lead, readout, held, local):
    hbm = pl.BlockSpec(memory_space=pltpu.HBM)
    vmem = pl.BlockSpec(memory_space=pltpu.VMEM)
    return pl.pallas_call(
        out_kernel,
        out_shape=jax.ShapeDtypeStruct((TOK, HEADS * HEAD_DIM), bf16),
        in_specs=[vmem, vmem, vmem, hbm],
        out_specs=hbm,
        scratch_shapes=[
            pltpu.VMEM((2, TOK, GROUP_COLS), f32),
            pltpu.VMEM((GROUPS, TOK, GROUP_COLS), bf16),
            pltpu.VMEM((GROUPS, TOK, GROUP_COLS), bf16),
            pltpu.SemaphoreType.DMA((GROUPS,)),
            pltpu.SemaphoreType.DMA((GROUPS,)),
        ],
        compiler_params=pltpu.CompilerParams(vmem_limit_bytes=OUT_VMEM_LIMIT),
        cost_estimate=pl.CostEstimate(
            flops=2_000_000_000, bytes_accessed=12_000_000, transcendentals=0
        ),
        name="outputs",
    )(lead, readout, held, local)


def swap_runs(v, bits, ways):
    return lax.ppermute(v, "seq", [(i, i ^ (bits * STEP)) for i in range(ways)])


def exchange(v, devices):
    return lax.all_to_all(
        v,
        ("seq", "head"),
        split_axis=0,
        concat_axis=0,
        tiled=True,
        axis_index_groups=[
            list(range(first, first + OWNERS)) for first in range(0, devices, OWNERS)
        ],
    )


def shards(features, step_size, log_decay, inject, readout, skip_gain):
    ways = lax.axis_size("seq")
    devices = ways * lax.axis_size("head")
    args = (features, step_size, log_decay, inject, readout, skip_gain[None, :])
    arrived = exchange(states_of(features, step_size, log_decay, inject), devices)
    local, lead = local_of(0, (), *args)
    arrived, local, lead = lax.optimization_barrier((arrived, local, lead))
    place = (lax.axis_index("seq") // STEP).astype(jnp.int32)[None]
    total = total_of(arrived)
    others = [swap_runs(total, bits, ways) for bits in (1, 2, 3)]
    held = held_of(place, others, arrived)
    held = exchange(held, devices)
    (local,) = local_of(1, (local,), *args)
    return outputs_of(lead, readout, held, local)


def solution(mesh):
    rows = P(("seq", "head"), None)
    return jax.shard_map(
        shards,
        mesh=mesh,
        in_specs=(rows, rows, rows, rows, rows, P()),
        out_specs=rows,
        check_vma=False,
    )
```

```python
import functools

import jax
import jax.numpy as jnp
from jax import lax
from jax.experimental import pallas as pl
from jax.experimental.pallas import tpu as pltpu
from jax.sharding import PartitionSpec as P

HEADS = 128
HEAD_DIM = 64
STATE = 128
GROUPS = 8
TOK = 256
HALF = 128
LANES = 128
OWNERS = 64
STEP = 4
PIECES = 8
OWN_HEADS = HEADS // OWNERS
COLS = OWN_HEADS * HEAD_DIM
GROUP_COLS = HEADS // GROUPS * HEAD_DIM
GROUP_OWNERS = OWNERS // GROUPS
ROWS = STATE + 8
VMEM_LIMIT = 61 * 1024 * 1024
OUT_VMEM_LIMIT = 50 * 1024 * 1024
HELD_VMEM_LIMIT = 40 * 1024 * 1024
SMALL_VMEM_LIMIT = 24 * 1024 * 1024
WIDE = 512
NARROW = 256
LOCAL_PARTS = 2
PART_GROUPS = GROUPS // LOCAL_PARTS
PART_COLS = PART_GROUPS * GROUP_COLS

f32 = jnp.float32
bf16 = jnp.bfloat16


def dot(a, b):
    return jnp.dot(a, b, preferred_element_type=f32)


def sums(mask, v):
    high = v.astype(bf16)
    rest = v - high.astype(f32)
    middle = rest.astype(bf16)
    low = (rest - middle.astype(f32)).astype(bf16)
    p = dot(mask.astype(bf16), jnp.concatenate([high, middle, low], axis=1))
    return p[:, :HEADS] + p[:, HEADS : 2 * HEADS] + p[:, 2 * HEADS :]


def iota(shape, axis):
    return lax.broadcasted_iota(jnp.int32, shape, axis)


def spread(scale, first_col, cols):
    place = iota((scale.shape[0], LANES), 1) >> 6
    first_head = first_col // HEAD_DIM
    return jnp.concatenate(
        [
            jnp.take_along_axis(
                scale, place + (first_head + 2 * k), axis=1, mode="promise_in_bounds"
            )
            for k in range(cols // LANES)
        ],
        axis=1,
    )


def copies(*triples):
    made = [pltpu.make_async_copy(*t) for t in triples]
    for c in made:
        c.start()
    return made


def state_kernel(
    x_hbm, step_hbm, decay_hbm, inject_hbm, out_hbm,
    x_buf, step_buf, decay_buf, inject_buf, turned_buf, v_buf, out_buf, sem, in_sem, out_sem,
):
    decay_in, step_in, inject_in = copies(
        (decay_hbm, decay_buf, sem.at[0]),
        (step_hbm, step_buf, sem.at[1]),
        (inject_hbm, inject_buf, sem.at[2]),
    )
    x_in = copies(
        *[
            (x_hbm.at[:, pl.ds(g * GROUP_COLS, GROUP_COLS)], x_buf.at[g], in_sem.at[g])
            for g in range(GROUPS)
        ]
    )
    later = jnp.where(iota((TOK, TOK), 1) > iota((TOK, TOK), 0), 1.0, 0.0).astype(f32)
    decay_in.wait()
    decay = decay_buf[...]
    tail = sums(later, decay)
    whole = jnp.broadcast_to(jnp.exp(tail[0:1] + decay[0:1]), (8, HEADS))
    high = whole.astype(bf16).astype(f32)
    row = iota((8, HEADS), 0)
    extra = jnp.where(row == 0, high, jnp.where(row == 1, whole - high, 0.0))
    step_in.wait()
    scale = step_buf[...] * jnp.exp(tail)
    inject_in.wait()
    for g in range(GROUPS):
        turned_buf[g] = inject_buf[:, g * STATE : (g + 1) * STATE].T
    sent = []
    for g in range(GROUPS + 1):
        if g < GROUPS:
            if g % 4 == 0:
                for c in x_in[g : g + 4]:
                    c.wait()
        first = (g - 1) * GROUP_OWNERS
        for w in range(GROUP_COLS // NARROW):
            part = slice(w * NARROW, (w + 1) * NARROW)
            if g < GROUPS:
                weight = spread(scale, g * GROUP_COLS + w * NARROW, NARROW)
                v_buf[g % 2, :, part] = x_buf[g, :, part] * weight.astype(bf16)
            if g > 0:
                s = dot(turned_buf[g - 1], v_buf[(g - 1) % 2, :, part]).astype(bf16)
                below = spread(extra, (g - 1) * GROUP_COLS + w * NARROW, NARROW).astype(bf16)
                for k in range(NARROW // COLS):
                    cols = slice(k * COLS, (k + 1) * COLS)
                    owner = first + w * (NARROW // COLS) + k
                    out_buf[owner, :STATE, :] = s[:, cols]
                    out_buf[owner, STATE:, :] = below[:, cols]
        if g > 0:
            span = pl.ds(first, GROUP_OWNERS)
            sent += copies((out_buf.at[span], out_hbm.at[span], out_sem.at[g - 1]))
    for c in sent:
        c.wait()


def states_of(x, step, decay, inject):
    hbm = pl.BlockSpec(memory_space=pltpu.HBM)
    return pl.pallas_call(
        state_kernel,
        out_shape=jax.ShapeDtypeStruct((OWNERS, ROWS, COLS), bf16),
        in_specs=[hbm] * 4,
        out_specs=hbm,
        scratch_shapes=[
            pltpu.VMEM((GROUPS, TOK, GROUP_COLS), bf16),
            pltpu.VMEM((TOK, HEADS), f32),
            pltpu.VMEM((TOK, HEADS), f32),
            pltpu.VMEM((TOK, GROUPS * STATE), bf16),
            pltpu.VMEM((GROUPS, STATE, TOK), bf16),
            pltpu.VMEM((2, TOK, GROUP_COLS), bf16),
            pltpu.VMEM((OWNERS, ROWS, COLS), bf16),
            pltpu.SemaphoreType.DMA((3,)),
            pltpu.SemaphoreType.DMA((GROUPS,)),
            pltpu.SemaphoreType.DMA((GROUPS,)),
        ],
        compiler_params=pltpu.CompilerParams(vmem_limit_bytes=VMEM_LIMIT),
        cost_estimate=pl.CostEstimate(
            flops=2_000_000_000, bytes_accessed=8_000_000, transcendentals=32768
        ),
        name="states",
    )(x, step, decay, inject)


def decay_row(block):
    return block[STATE : STATE + 1].astype(f32) + block[STATE + 1 : STATE + 2].astype(f32)


def pack_rows(decay):
    row = iota((8, COLS), 0)
    high = decay.astype(bf16).astype(f32)
    return jnp.where(row == 0, high, jnp.where(row == 1, decay - high, 0.0)).astype(bf16)


def total_kernel(in_ref, out_ref):
    state = in_ref[0, :STATE, :].astype(f32)
    decay = decay_row(in_ref[0])
    for i in range(1, OWNERS):
        d = decay_row(in_ref[i])
        state = state * d + in_ref[i, :STATE, :].astype(f32)
        decay = decay * d
    out_ref[:STATE, :] = state.astype(bf16)
    out_ref[STATE:, :] = pack_rows(decay)


def join_kernel(place_ref, own_ref, other_ref, pair_ref):
    second = place_ref[0] % 2 == 1
    own, other = own_ref[...].astype(f32), other_ref[...].astype(f32)
    late = jnp.where(second, own, other)
    early = jnp.where(second, other, own)
    late_decay, early_decay = decay_row(late), decay_row(early)
    pair_ref[:STATE, :] = (late[:STATE] + late_decay * early[:STATE]).astype(bf16)
    pair_ref[STATE:, :] = pack_rows(late_decay * early_decay)


def held_kernel(place_ref, other_ref, pair_ref, in_ref, out_hbm, out_buf, sem):
    place = place_ref[0]
    state = jnp.where(place >= 2, pair_ref[:STATE, :].astype(f32), 0.0)
    other = other_ref[...].astype(f32)
    state = jnp.where(place % 2 == 1, other[:STATE] + decay_row(other) * state, state)
    size = OWNERS // PIECES
    sent = []
    for i in range(OWNERS):
        out_buf[i] = state.astype(bf16)
        if (i + 1) % size == 0:
            span = pl.ds(i + 1 - size, size)
            sent += copies((out_buf.at[span], out_hbm.at[span], sem.at[i // size]))
        if i + 1 < OWNERS:
            state = state * decay_row(in_ref[i]) + in_ref[i, :STATE, :].astype(f32)
    for c in sent:
        c.wait()


def total_of(arrived):
    return pl.pallas_call(
        total_kernel,
        out_shape=jax.ShapeDtypeStruct((ROWS, COLS), bf16),
        compiler_params=pltpu.CompilerParams(vmem_limit_bytes=SMALL_VMEM_LIMIT),
        cost_estimate=pl.CostEstimate(flops=4_000_000, bytes_accessed=2_000_000, transcendentals=0),
        name="total",
    )(arrived)


def pair_of(place, own, other):
    vmem = pl.BlockSpec(memory_space=pltpu.VMEM)
    return pl.pallas_call(
        join_kernel,
        out_shape=jax.ShapeDtypeStruct((ROWS, COLS), bf16),
        in_specs=[pl.BlockSpec(memory_space=pltpu.SMEM), vmem, vmem],
        compiler_params=pltpu.CompilerParams(vmem_limit_bytes=SMALL_VMEM_LIMIT),
        cost_estimate=pl.CostEstimate(flops=100_000, bytes_accessed=100_000, transcendentals=0),
        name="pair",
    )(place, own, other)


def held_of(place, other, pair, arrived):
    vmem = pl.BlockSpec(memory_space=pltpu.VMEM)
    return pl.pallas_call(
        held_kernel,
        out_shape=pltpu.HBM((OWNERS, STATE, COLS), bf16),
        in_specs=[pl.BlockSpec(memory_space=pltpu.SMEM), vmem, vmem, vmem],
        out_specs=pl.BlockSpec(memory_space=pltpu.HBM),
        scratch_shapes=[
            pltpu.VMEM((OWNERS, STATE, COLS), bf16),
            pltpu.SemaphoreType.DMA((PIECES,)),
        ],
        compiler_params=pltpu.CompilerParams(vmem_limit_bytes=HELD_VMEM_LIMIT),
        cost_estimate=pl.CostEstimate(flops=4_000_000, bytes_accessed=4_000_000, transcendentals=0),
        name="held",
    )(place, other, pair, arrived)


def local_kernel(
    part, x_hbm, step_hbm, decay_hbm, inject_hbm, readout_hbm, gain_ref, *rest
):
    if part == 0:
        out_hbm, lead_ref = rest[:2]
    else:
        out_hbm = rest[1]
    x_buf, step_buf, decay_buf, inject_buf, readout_buf, out_buf, sem, in_sem, out_sem = rest[2:]
    decay_in, step_in, inject_in, readout_in = copies(
        (decay_hbm, decay_buf, sem.at[0]),
        (step_hbm, step_buf, sem.at[1]),
        (inject_hbm, inject_buf, sem.at[2]),
        (readout_hbm, readout_buf, sem.at[3]),
    )
    x_in = copies(
        *[
            (
                x_hbm.at[:, pl.ds(part * PART_COLS + n * GROUP_COLS, GROUP_COLS)],
                x_buf.at[n],
                in_sem.at[n],
            )
            for n in range(PART_GROUPS)
        ]
    )
    lower = iota((HALF, HALF), 0) >= iota((HALF, HALF), 1)
    lower_f = jnp.where(lower, 1.0, 0.0).astype(f32)
    decay_in.wait()
    cum_a = sums(lower_f, decay_buf[:HALF])
    cum_b = sums(lower_f, decay_buf[HALF:])
    if part == 0:
        lead_ref[:HALF] = jnp.exp(cum_a)
        lead_ref[HALF:] = jnp.exp(cum_b + cum_a[HALF - 1 : HALF])
    mid = HALF // 2 - 1
    mid_b = cum_b[mid : mid + 1]
    gap_a = cum_a - cum_a[mid : mid + 1]
    gap_b = cum_b - mid_b
    onward = jnp.exp(mid_b + gap_a[HALF - 1 : HALF])
    few = iota((8, HEADS), 0)
    rows = jnp.where(few == 0, onward, gain_ref[...])
    step_in.wait()
    into_a = step_buf[:HALF] * jnp.exp(-gap_a)
    into_b = step_buf[HALF:] * jnp.exp(-gap_b)
    from_a = jnp.exp(gap_a)
    from_b = jnp.exp(gap_b)
    zero = jnp.zeros((HALF, HALF), f32)
    inject_in.wait()
    readout_in.wait()

    def pair(r, i):
        return lax.dot_general(r, i, (((1,), (1,)), ((), ())), preferred_element_type=f32)

    sent = []
    for n in range(PART_GROUPS):
        g = part * PART_GROUPS + n
        state_cols = slice(g * STATE, (g + 1) * STATE)
        inj_a = inject_buf[:HALF, state_cols]
        inj_b = inject_buf[HALF:, state_cols]
        read_a = readout_buf[:HALF, state_cols]
        read_b = readout_buf[HALF:, state_cols]
        near_a = jnp.where(lower, pair(read_a, inj_a), zero).astype(bf16)
        near_b = jnp.concatenate(
            [
                pair(read_b, inj_a).astype(bf16),
                jnp.where(lower, pair(read_b, inj_b), zero).astype(bf16),
            ],
            axis=1,
        )
        x_in[n].wait()
        for k in range(GROUP_COLS // WIDE):
            cols = slice(k * WIDE, (k + 1) * WIDE)
            at = g * GROUP_COLS + k * WIDE
            row = spread(rows, at, WIDE)
            gain = row[1:2]
            x_a = x_buf[n, :HALF, cols].astype(f32)
            x_b = x_buf[n, HALF:, cols].astype(f32)
            v_a = x_a * spread(into_a, at, WIDE)
            v_b = (x_b * spread(into_b, at, WIDE)).astype(bf16)
            res_a = dot(near_a, v_a.astype(bf16))
            res_b = dot(near_b, jnp.concatenate([(v_a * row[0:1]).astype(bf16), v_b], axis=0))
            out_a = res_a * spread(from_a, at, WIDE) + gain * x_a
            out_b = res_b * spread(from_b, at, WIDE) + gain * x_b
            out_buf[n, :HALF, cols] = out_a.astype(bf16)
            out_buf[n, HALF:, cols] = out_b.astype(bf16)
        sent += copies(
            (out_buf.at[n], out_hbm.at[:, pl.ds(g * GROUP_COLS, GROUP_COLS)], out_sem.at[n])
        )
    for c in sent:
        c.wait()


def local_of(part, so_far, x, step, decay, inject, readout, gain):
    hbm = pl.BlockSpec(memory_space=pltpu.HBM)
    vmem = pl.BlockSpec(memory_space=pltpu.VMEM)
    return pl.pallas_call(
        functools.partial(local_kernel, part),
        out_shape=[jax.ShapeDtypeStruct(x.shape, bf16)]
        + ([] if so_far else [jax.ShapeDtypeStruct((TOK, HEADS), f32)]),
        in_specs=[hbm] * 5 + [vmem] + [hbm] * len(so_far),
        input_output_aliases={6: 0} if so_far else {},
        out_specs=[hbm] if so_far else [hbm, vmem],
        scratch_shapes=[
            pltpu.VMEM((PART_GROUPS, TOK, GROUP_COLS), bf16),
            pltpu.VMEM((TOK, HEADS), f32),
            pltpu.VMEM((TOK, HEADS), f32),
            pltpu.VMEM((TOK, GROUPS * STATE), bf16),
            pltpu.VMEM((TOK, GROUPS * STATE), bf16),
            pltpu.VMEM((PART_GROUPS, TOK, GROUP_COLS), bf16),
            pltpu.SemaphoreType.DMA((4,)),
            pltpu.SemaphoreType.DMA((PART_GROUPS,)),
            pltpu.SemaphoreType.DMA((PART_GROUPS,)),
        ],
        compiler_params=pltpu.CompilerParams(vmem_limit_bytes=VMEM_LIMIT),
        cost_estimate=pl.CostEstimate(
            flops=2_000_000_000, bytes_accessed=6_000_000, transcendentals=65536
        ),
        name=f"local{part}",
    )(x, step, decay, inject, readout, gain, *so_far)


def out_kernel(
    lead_ref, readout_ref, held_ref, local_hbm, out_hbm, far_buf, local_buf, out_buf, local_sem, out_sem
):
    local_in = copies(
        *[
            (local_hbm.at[:, pl.ds(g * GROUP_COLS, GROUP_COLS)], local_buf.at[g], local_sem.at[g])
            for g in range(GROUPS)
        ]
    )
    sent = []
    for g in range(GROUPS + 1):
        if g % 2 == 1:
            local_in[g - 1].wait()
            local_in[g].wait()
        if g < GROUPS:
            held = jnp.concatenate(
                [held_ref[g * GROUP_OWNERS + i] for i in range(GROUP_OWNERS)], axis=1
            )
            far_buf[g % 2] = dot(readout_ref[:, g * STATE : (g + 1) * STATE], held).astype(bf16)
        if g > 0:
            at = (g - 1) * GROUP_COLS
            lead = spread(lead_ref[...], at, GROUP_COLS).astype(bf16)
            out_buf[g - 1] = far_buf[(g - 1) % 2] * lead + local_buf[g - 1]
            sent += copies(
                (out_buf.at[g - 1], out_hbm.at[:, pl.ds(at, GROUP_COLS)], out_sem.at[g - 1])
            )
    for c in sent:
        c.wait()


def outputs_of(lead, readout, held, local):
    hbm = pl.BlockSpec(memory_space=pltpu.HBM)
    vmem = pl.BlockSpec(memory_space=pltpu.VMEM)
    return pl.pallas_call(
        out_kernel,
        out_shape=jax.ShapeDtypeStruct((TOK, HEADS * HEAD_DIM), bf16),
        in_specs=[vmem, vmem, vmem, hbm],
        out_specs=hbm,
        scratch_shapes=[
            pltpu.VMEM((2, TOK, GROUP_COLS), bf16),
            pltpu.VMEM((GROUPS, TOK, GROUP_COLS), bf16),
            pltpu.VMEM((GROUPS, TOK, GROUP_COLS), bf16),
            pltpu.SemaphoreType.DMA((GROUPS,)),
            pltpu.SemaphoreType.DMA((GROUPS,)),
        ],
        compiler_params=pltpu.CompilerParams(vmem_limit_bytes=OUT_VMEM_LIMIT),
        cost_estimate=pl.CostEstimate(
            flops=2_000_000_000, bytes_accessed=12_000_000, transcendentals=0
        ),
        name="outputs",
    )(lead, readout, held, local)


def swap_runs(v, bits, ways):
    return lax.ppermute(v, "seq", [(i, i ^ (bits * STEP)) for i in range(ways)])


def exchange(v, devices):
    return lax.all_to_all(
        v,
        ("seq", "head"),
        split_axis=0,
        concat_axis=0,
        tiled=True,
        axis_index_groups=[
            list(range(first, first + OWNERS)) for first in range(0, devices, OWNERS)
        ],
    )


def shards(features, step_size, log_decay, inject, readout, skip_gain):
    ways = lax.axis_size("seq")
    devices = ways * lax.axis_size("head")
    args = (features, step_size, log_decay, inject, readout, skip_gain[None, :])
    arrived = exchange(states_of(features, step_size, log_decay, inject), devices)
    local, lead = local_of(0, (), *args)
    arrived, local, lead = lax.optimization_barrier((arrived, local, lead))
    place = (lax.axis_index("seq") // STEP).astype(jnp.int32)[None]
    total = total_of(arrived)
    other = swap_runs(total, 1, ways)
    pair = swap_runs(pair_of(place, total, other), 3, ways)
    held = held_of(place, other, pair, arrived)
    held = exchange(held, devices)
    (local,) = local_of(1, (local,), *args)
    return outputs_of(lead, readout, held, local)


def solution(mesh):
    rows = P(("seq", "head"), None)
    return jax.shard_map(
        shards,
        mesh=mesh,
        in_specs=(rows, rows, rows, rows, rows, P()),
        out_specs=rows,
        check_vma=False,
    )
```

```python
import functools

import jax
import jax.numpy as jnp
from jax import lax
from jax.experimental import pallas as pl
from jax.experimental.pallas import tpu as pltpu
from jax.sharding import PartitionSpec as P

HEADS = 128
HEAD_DIM = 64
STATE = 128
GROUPS = 8
TOK = 256
HALF = 128
LANES = 128
OWNERS = 64
STEP = 4
PIECES = 8
OWN_HEADS = HEADS // OWNERS
COLS = OWN_HEADS * HEAD_DIM
GROUP_COLS = HEADS // GROUPS * HEAD_DIM
GROUP_OWNERS = OWNERS // GROUPS
ROWS = STATE + 8
VMEM_LIMIT = 61 * 1024 * 1024
OUT_VMEM_LIMIT = 50 * 1024 * 1024
HELD_VMEM_LIMIT = 40 * 1024 * 1024
SMALL_VMEM_LIMIT = 24 * 1024 * 1024
WIDE = 512
NARROW = 256
LOCAL_PARTS = 2
PART_GROUPS = GROUPS // LOCAL_PARTS
PART_COLS = PART_GROUPS * GROUP_COLS

f32 = jnp.float32
bf16 = jnp.bfloat16


def dot(a, b):
    return jnp.dot(a, b, preferred_element_type=f32)


def sums(mask, v):
    high = v.astype(bf16)
    rest = v - high.astype(f32)
    middle = rest.astype(bf16)
    low = (rest - middle.astype(f32)).astype(bf16)
    p = dot(mask.astype(bf16), jnp.concatenate([high, middle, low], axis=1))
    return p[:, :HEADS] + p[:, HEADS : 2 * HEADS] + p[:, 2 * HEADS :]


def iota(shape, axis):
    return lax.broadcasted_iota(jnp.int32, shape, axis)


def spread(scale, first_col, cols):
    place = iota((scale.shape[0], LANES), 1) >> 6
    first_head = first_col // HEAD_DIM
    return jnp.concatenate(
        [
            jnp.take_along_axis(
                scale, place + (first_head + 2 * k), axis=1, mode="promise_in_bounds"
            )
            for k in range(cols // LANES)
        ],
        axis=1,
    )


def copies(*triples):
    made = [pltpu.make_async_copy(*t) for t in triples]
    for c in made:
        c.start()
    return made


def state_kernel(
    x_hbm, step_hbm, decay_hbm, inject_hbm, out_hbm,
    x_buf, step_buf, decay_buf, inject_buf, turned_buf, v_buf, out_buf, sem, in_sem, out_sem,
):
    decay_in, step_in, inject_in = copies(
        (decay_hbm, decay_buf, sem.at[0]),
        (step_hbm, step_buf, sem.at[1]),
        (inject_hbm, inject_buf, sem.at[2]),
    )
    x_in = copies(
        *[
            (x_hbm.at[:, pl.ds(g * GROUP_COLS, GROUP_COLS)], x_buf.at[g], in_sem.at[g])
            for g in range(GROUPS)
        ]
    )
    later = jnp.where(iota((TOK, TOK), 1) > iota((TOK, TOK), 0), 1.0, 0.0).astype(f32)
    decay_in.wait()
    decay = decay_buf[...]
    tail = sums(later, decay)
    whole = jnp.broadcast_to(jnp.exp(tail[0:1] + decay[0:1]), (8, HEADS))
    high = whole.astype(bf16).astype(f32)
    row = iota((8, HEADS), 0)
    extra = jnp.where(row == 0, high, jnp.where(row == 1, whole - high, 0.0))
    step_in.wait()
    scale = step_buf[...] * jnp.exp(tail)
    inject_in.wait()
    for g in range(GROUPS):
        turned_buf[g] = inject_buf[:, g * STATE : (g + 1) * STATE].T
    sent = []
    for g in range(GROUPS + 1):
        if g < GROUPS:
            if g % 4 == 0:
                for c in x_in[g : g + 4]:
                    c.wait()
        first = (g - 1) * GROUP_OWNERS
        for w in range(GROUP_COLS // NARROW):
            part = slice(w * NARROW, (w + 1) * NARROW)
            if g < GROUPS:
                weight = spread(scale, g * GROUP_COLS + w * NARROW, NARROW)
                v_buf[g % 2, :, part] = x_buf[g, :, part] * weight.astype(bf16)
            if g > 0:
                s = dot(turned_buf[g - 1], v_buf[(g - 1) % 2, :, part]).astype(bf16)
                below = spread(extra, (g - 1) * GROUP_COLS + w * NARROW, NARROW).astype(bf16)
                for k in range(NARROW // COLS):
                    cols = slice(k * COLS, (k + 1) * COLS)
                    owner = first + w * (NARROW // COLS) + k
                    out_buf[owner, :STATE, :] = s[:, cols]
                    out_buf[owner, STATE:, :] = below[:, cols]
        if g > 0:
            span = pl.ds(first, GROUP_OWNERS)
            sent += copies((out_buf.at[span], out_hbm.at[span], out_sem.at[g - 1]))
    for c in sent:
        c.wait()


def states_of(x, step, decay, inject):
    hbm = pl.BlockSpec(memory_space=pltpu.HBM)
    return pl.pallas_call(
        state_kernel,
        out_shape=jax.ShapeDtypeStruct((OWNERS, ROWS, COLS), bf16),
        in_specs=[hbm] * 4,
        out_specs=hbm,
        scratch_shapes=[
            pltpu.VMEM((GROUPS, TOK, GROUP_COLS), bf16),
            pltpu.VMEM((TOK, HEADS), f32),
            pltpu.VMEM((TOK, HEADS), f32),
            pltpu.VMEM((TOK, GROUPS * STATE), bf16),
            pltpu.VMEM((GROUPS, STATE, TOK), bf16),
            pltpu.VMEM((2, TOK, GROUP_COLS), bf16),
            pltpu.VMEM((OWNERS, ROWS, COLS), bf16),
            pltpu.SemaphoreType.DMA((3,)),
            pltpu.SemaphoreType.DMA((GROUPS,)),
            pltpu.SemaphoreType.DMA((GROUPS,)),
        ],
        compiler_params=pltpu.CompilerParams(vmem_limit_bytes=VMEM_LIMIT),
        cost_estimate=pl.CostEstimate(
            flops=2_000_000_000, bytes_accessed=8_000_000, transcendentals=32768
        ),
        name="states",
    )(x, step, decay, inject)


def decay_row(block):
    return block[STATE : STATE + 1].astype(f32) + block[STATE + 1 : STATE + 2].astype(f32)


def pack_rows(decay):
    row = iota((8, COLS), 0)
    high = decay.astype(bf16).astype(f32)
    return jnp.where(row == 0, high, jnp.where(row == 1, decay - high, 0.0)).astype(bf16)


def total_kernel(in_ref, out_ref):
    state = in_ref[0, :STATE, :].astype(f32)
    decay = decay_row(in_ref[0])
    for i in range(1, OWNERS):
        d = decay_row(in_ref[i])
        state = state * d + in_ref[i, :STATE, :].astype(f32)
        decay = decay * d
    out_ref[:STATE, :] = state.astype(bf16)
    out_ref[STATE:, :] = pack_rows(decay)


def join_kernel(place_ref, own_ref, other_ref, pair_ref):
    second = place_ref[0] % 2 == 1
    own, other = own_ref[...].astype(f32), other_ref[...].astype(f32)
    late = jnp.where(second, own, other)
    early = jnp.where(second, other, own)
    late_decay, early_decay = decay_row(late), decay_row(early)
    pair_ref[:STATE, :] = (late[:STATE] + late_decay * early[:STATE]).astype(bf16)
    pair_ref[STATE:, :] = pack_rows(late_decay * early_decay)


def held_kernel(place_ref, other_ref, pair_ref, in_ref, out_hbm, out_buf, sem):
    place = place_ref[0]
    state = jnp.where(place >= 2, pair_ref[:STATE, :].astype(f32), 0.0)
    other = other_ref[...].astype(f32)
    state = jnp.where(place % 2 == 1, other[:STATE] + decay_row(other) * state, state)
    size = OWNERS // PIECES
    sent = []
    for i in range(OWNERS):
        out_buf[i] = state.astype(bf16)
        if (i + 1) % size == 0:
            span = pl.ds(i + 1 - size, size)
            sent += copies((out_buf.at[span], out_hbm.at[span], sem.at[i // size]))
        if i + 1 < OWNERS:
            state = state * decay_row(in_ref[i]) + in_ref[i, :STATE, :].astype(f32)
    for c in sent:
        c.wait()


def total_of(arrived):
    return pl.pallas_call(
        total_kernel,
        out_shape=jax.ShapeDtypeStruct((ROWS, COLS), bf16),
        compiler_params=pltpu.CompilerParams(vmem_limit_bytes=SMALL_VMEM_LIMIT),
        cost_estimate=pl.CostEstimate(flops=4_000_000, bytes_accessed=2_000_000, transcendentals=0),
        name="total",
    )(arrived)


def pair_of(place, own, other):
    vmem = pl.BlockSpec(memory_space=pltpu.VMEM)
    return pl.pallas_call(
        join_kernel,
        out_shape=jax.ShapeDtypeStruct((ROWS, COLS), bf16),
        in_specs=[pl.BlockSpec(memory_space=pltpu.SMEM), vmem, vmem],
        compiler_params=pltpu.CompilerParams(vmem_limit_bytes=SMALL_VMEM_LIMIT),
        cost_estimate=pl.CostEstimate(flops=100_000, bytes_accessed=100_000, transcendentals=0),
        name="pair",
    )(place, own, other)


def held_of(place, other, pair, arrived):
    vmem = pl.BlockSpec(memory_space=pltpu.VMEM)
    return pl.pallas_call(
        held_kernel,
        out_shape=pltpu.HBM((OWNERS, STATE, COLS), bf16),
        in_specs=[pl.BlockSpec(memory_space=pltpu.SMEM), vmem, vmem, vmem],
        out_specs=pl.BlockSpec(memory_space=pltpu.HBM),
        scratch_shapes=[
            pltpu.VMEM((OWNERS, STATE, COLS), bf16),
            pltpu.SemaphoreType.DMA((PIECES,)),
        ],
        compiler_params=pltpu.CompilerParams(vmem_limit_bytes=HELD_VMEM_LIMIT),
        cost_estimate=pl.CostEstimate(flops=4_000_000, bytes_accessed=4_000_000, transcendentals=0),
        name="held",
    )(place, other, pair, arrived)


def local_kernel(
    part, x_hbm, step_hbm, decay_hbm, inject_hbm, readout_hbm, gain_ref, *rest
):
    if part == 0:
        out_hbm, lead_ref = rest[:2]
    else:
        out_hbm = rest[1]
    x_buf, step_buf, decay_buf, inject_buf, readout_buf, out_buf, sem, in_sem, out_sem = rest[2:]
    decay_in, step_in, inject_in, readout_in = copies(
        (decay_hbm, decay_buf, sem.at[0]),
        (step_hbm, step_buf, sem.at[1]),
        (inject_hbm, inject_buf, sem.at[2]),
        (readout_hbm, readout_buf, sem.at[3]),
    )
    x_in = copies(
        *[
            (
                x_hbm.at[:, pl.ds(part * PART_COLS + n * GROUP_COLS, GROUP_COLS)],
                x_buf.at[n],
                in_sem.at[n],
            )
            for n in range(PART_GROUPS)
        ]
    )
    lower = iota((HALF, HALF), 0) >= iota((HALF, HALF), 1)
    lower_f = jnp.where(lower, 1.0, 0.0).astype(f32)
    decay_in.wait()
    cum_a = sums(lower_f, decay_buf[:HALF])
    cum_b = sums(lower_f, decay_buf[HALF:])
    if part == 0:
        lead_ref[:HALF] = jnp.exp(cum_a)
        lead_ref[HALF:] = jnp.exp(cum_b + cum_a[HALF - 1 : HALF])
    mid = HALF // 2 - 1
    mid_b = cum_b[mid : mid + 1]
    gap_a = cum_a - cum_a[mid : mid + 1]
    gap_b = cum_b - mid_b
    onward = jnp.exp(mid_b + gap_a[HALF - 1 : HALF])
    few = iota((8, HEADS), 0)
    rows = jnp.where(few == 0, onward, gain_ref[...])
    step_in.wait()
    into_a = step_buf[:HALF] * jnp.exp(-gap_a)
    into_b = step_buf[HALF:] * jnp.exp(-gap_b)
    from_a = jnp.exp(gap_a)
    from_b = jnp.exp(gap_b)
    zero = jnp.zeros((HALF, HALF), f32)
    inject_in.wait()
    readout_in.wait()

    def pair(r, i):
        return lax.dot_general(r, i, (((1,), (1,)), ((), ())), preferred_element_type=f32)

    sent = []
    for n in range(PART_GROUPS):
        g = part * PART_GROUPS + n
        state_cols = slice(g * STATE, (g + 1) * STATE)
        inj_a = inject_buf[:HALF, state_cols]
        inj_b = inject_buf[HALF:, state_cols]
        read_a = readout_buf[:HALF, state_cols]
        read_b = readout_buf[HALF:, state_cols]
        near_a = jnp.where(lower, pair(read_a, inj_a), zero).astype(bf16)
        near_b = jnp.concatenate(
            [
                pair(read_b, inj_a).astype(bf16),
                jnp.where(lower, pair(read_b, inj_b), zero).astype(bf16),
            ],
            axis=1,
        )
        x_in[n].wait()
        for k in range(GROUP_COLS // WIDE):
            cols = slice(k * WIDE, (k + 1) * WIDE)
            at = g * GROUP_COLS + k * WIDE
            row = spread(rows, at, WIDE)
            gain = row[1:2]
            x_a = x_buf[n, :HALF, cols].astype(f32)
            x_b = x_buf[n, HALF:, cols].astype(f32)
            v_a = x_a * spread(into_a, at, WIDE)
            v_b = (x_b * spread(into_b, at, WIDE)).astype(bf16)
            res_a = dot(near_a, v_a.astype(bf16))
            res_b = dot(near_b, jnp.concatenate([(v_a * row[0:1]).astype(bf16), v_b], axis=0))
            out_a = res_a * spread(from_a, at, WIDE) + gain * x_a
            out_b = res_b * spread(from_b, at, WIDE) + gain * x_b
            out_buf[n, :HALF, cols] = out_a.astype(bf16)
            out_buf[n, HALF:, cols] = out_b.astype(bf16)
        sent += copies(
            (out_buf.at[n], out_hbm.at[:, pl.ds(g * GROUP_COLS, GROUP_COLS)], out_sem.at[n])
        )
    for c in sent:
        c.wait()


def local_of(part, so_far, x, step, decay, inject, readout, gain):
    hbm = pl.BlockSpec(memory_space=pltpu.HBM)
    vmem = pl.BlockSpec(memory_space=pltpu.VMEM)
    return pl.pallas_call(
        functools.partial(local_kernel, part),
        out_shape=[jax.ShapeDtypeStruct(x.shape, bf16)]
        + ([] if so_far else [jax.ShapeDtypeStruct((TOK, HEADS), f32)]),
        in_specs=[hbm] * 5 + [vmem] + [hbm] * len(so_far),
        input_output_aliases={6: 0} if so_far else {},
        out_specs=[hbm] if so_far else [hbm, vmem],
        scratch_shapes=[
            pltpu.VMEM((PART_GROUPS, TOK, GROUP_COLS), bf16),
            pltpu.VMEM((TOK, HEADS), f32),
            pltpu.VMEM((TOK, HEADS), f32),
            pltpu.VMEM((TOK, GROUPS * STATE), bf16),
            pltpu.VMEM((TOK, GROUPS * STATE), bf16),
            pltpu.VMEM((PART_GROUPS, TOK, GROUP_COLS), bf16),
            pltpu.SemaphoreType.DMA((4,)),
            pltpu.SemaphoreType.DMA((PART_GROUPS,)),
            pltpu.SemaphoreType.DMA((PART_GROUPS,)),
        ],
        compiler_params=pltpu.CompilerParams(vmem_limit_bytes=VMEM_LIMIT),
        cost_estimate=pl.CostEstimate(
            flops=2_000_000_000, bytes_accessed=6_000_000, transcendentals=65536
        ),
        name=f"local{part}",
    )(x, step, decay, inject, readout, gain, *so_far)


def out_kernel(
    lead_ref, readout_ref, held_ref, local_hbm, out_hbm, far_buf, local_buf, out_buf, local_sem, out_sem
):
    local_in = copies(
        *[
            (local_hbm.at[:, pl.ds(g * GROUP_COLS, GROUP_COLS)], local_buf.at[g], local_sem.at[g])
            for g in range(GROUPS)
        ]
    )
    sent = []
    for g in range(GROUPS + 1):
        if g % 2 == 1:
            local_in[g - 1].wait()
            local_in[g].wait()
        if g < GROUPS:
            held = jnp.concatenate(
                [held_ref[g * GROUP_OWNERS + i] for i in range(GROUP_OWNERS)], axis=1
            )
            far_buf[g % 2] = dot(readout_ref[:, g * STATE : (g + 1) * STATE], held).astype(bf16)
        if g > 0:
            at = (g - 1) * GROUP_COLS
            lead = spread(lead_ref[...], at, GROUP_COLS).astype(bf16)
            out_buf[g - 1] = far_buf[(g - 1) % 2] * lead + local_buf[g - 1]
            sent += copies(
                (out_buf.at[g - 1], out_hbm.at[:, pl.ds(at, GROUP_COLS)], out_sem.at[g - 1])
            )
    for c in sent:
        c.wait()


def outputs_of(lead, readout, held, local):
    hbm = pl.BlockSpec(memory_space=pltpu.HBM)
    vmem = pl.BlockSpec(memory_space=pltpu.VMEM)
    return pl.pallas_call(
        out_kernel,
        out_shape=jax.ShapeDtypeStruct((TOK, HEADS * HEAD_DIM), bf16),
        in_specs=[vmem, vmem, vmem, hbm],
        out_specs=hbm,
        scratch_shapes=[
            pltpu.VMEM((2, TOK, GROUP_COLS), bf16),
            pltpu.VMEM((GROUPS, TOK, GROUP_COLS), bf16),
            pltpu.VMEM((GROUPS, TOK, GROUP_COLS), bf16),
            pltpu.SemaphoreType.DMA((GROUPS,)),
            pltpu.SemaphoreType.DMA((GROUPS,)),
        ],
        compiler_params=pltpu.CompilerParams(vmem_limit_bytes=OUT_VMEM_LIMIT),
        cost_estimate=pl.CostEstimate(
            flops=2_000_000_000, bytes_accessed=12_000_000, transcendentals=0
        ),
        name="outputs",
    )(lead, readout, held, local)


def swap_runs(v, bits, ways):
    return lax.ppermute(v, "seq", [(i, i ^ (bits * STEP)) for i in range(ways)])


def exchange(v, devices):
    return lax.all_to_all(
        v,
        ("seq", "head"),
        split_axis=0,
        concat_axis=0,
        tiled=True,
        axis_index_groups=[
            list(range(first, first + OWNERS)) for first in range(0, devices, OWNERS)
        ],
    )


def shards(features, step_size, log_decay, inject, readout, skip_gain):
    ways = lax.axis_size("seq")
    devices = ways * lax.axis_size("head")
    args = (features, step_size, log_decay, inject, readout, skip_gain[None, :])
    arrived = exchange(states_of(features, step_size, log_decay, inject), devices)
    local, lead = local_of(0, (), *args)
    (local,) = local_of(1, (local,), *args)
    arrived, local, lead = lax.optimization_barrier((arrived, local, lead))
    place = (lax.axis_index("seq") // STEP).astype(jnp.int32)[None]
    total = total_of(arrived)
    other = swap_runs(total, 1, ways)
    pair = swap_runs(pair_of(place, total, other), 3, ways)
    held = held_of(place, other, pair, arrived)
    held = exchange(held, devices)
    return outputs_of(lead, readout, held, local)


def solution(mesh):
    rows = P(("seq", "head"), None)
    return jax.shard_map(
        shards,
        mesh=mesh,
        in_specs=(rows, rows, rows, rows, rows, P()),
        out_specs=rows,
        check_vma=False,
    )
```

```python
import functools

import jax
import jax.numpy as jnp
from jax import lax
from jax.experimental import pallas as pl
from jax.experimental.pallas import tpu as pltpu
from jax.sharding import PartitionSpec as P

HEADS = 128
HEAD_DIM = 64
STATE = 128
GROUPS = 8
TOK = 256
HALF = 128
LANES = 128
OWNERS = 64
STEP = 4
PIECES = 8
OWN_HEADS = HEADS // OWNERS
COLS = OWN_HEADS * HEAD_DIM
GROUP_COLS = HEADS // GROUPS * HEAD_DIM
GROUP_OWNERS = OWNERS // GROUPS
ROWS = STATE + 8
VMEM_LIMIT = 61 * 1024 * 1024
OUT_VMEM_LIMIT = 50 * 1024 * 1024
HELD_VMEM_LIMIT = 40 * 1024 * 1024
SMALL_VMEM_LIMIT = 24 * 1024 * 1024
WIDE = 512
NARROW = 256
LOCAL_PARTS = 2
PART_GROUPS = GROUPS // LOCAL_PARTS
PART_COLS = PART_GROUPS * GROUP_COLS

f32 = jnp.float32
bf16 = jnp.bfloat16


def dot(a, b):
    return jnp.dot(a, b, preferred_element_type=f32)


def sums(mask, v):
    high = v.astype(bf16)
    rest = v - high.astype(f32)
    middle = rest.astype(bf16)
    low = (rest - middle.astype(f32)).astype(bf16)
    p = dot(mask.astype(bf16), jnp.concatenate([high, middle, low], axis=1))
    return p[:, :HEADS] + p[:, HEADS : 2 * HEADS] + p[:, 2 * HEADS :]


def iota(shape, axis):
    return lax.broadcasted_iota(jnp.int32, shape, axis)


def spread(scale, first_col, cols):
    place = iota((scale.shape[0], LANES), 1) >> 6
    first_head = first_col // HEAD_DIM
    return jnp.concatenate(
        [
            jnp.take_along_axis(
                scale, place + (first_head + 2 * k), axis=1, mode="promise_in_bounds"
            )
            for k in range(cols // LANES)
        ],
        axis=1,
    )


def copies(*triples):
    made = [pltpu.make_async_copy(*t) for t in triples]
    for c in made:
        c.start()
    return made


def state_kernel(
    x_hbm, step_hbm, decay_hbm, inject_hbm, out_hbm,
    x_buf, step_buf, decay_buf, inject_buf, turned_buf, v_buf, out_buf, sem, in_sem, out_sem,
):
    decay_in, step_in, inject_in = copies(
        (decay_hbm, decay_buf, sem.at[0]),
        (step_hbm, step_buf, sem.at[1]),
        (inject_hbm, inject_buf, sem.at[2]),
    )
    x_in = copies(
        *[
            (x_hbm.at[:, pl.ds(g * GROUP_COLS, GROUP_COLS)], x_buf.at[g], in_sem.at[g])
            for g in range(GROUPS)
        ]
    )
    later = jnp.where(iota((TOK, TOK), 1) > iota((TOK, TOK), 0), 1.0, 0.0).astype(f32)
    decay_in.wait()
    decay = decay_buf[...]
    tail = sums(later, decay)
    whole = jnp.broadcast_to(jnp.exp(tail[0:1] + decay[0:1]), (8, HEADS))
    high = whole.astype(bf16).astype(f32)
    row = iota((8, HEADS), 0)
    extra = jnp.where(row == 0, high, jnp.where(row == 1, whole - high, 0.0))
    step_in.wait()
    scale = step_buf[...] * jnp.exp(tail)
    inject_in.wait()
    for g in range(GROUPS):
        turned_buf[g] = inject_buf[:, g * STATE : (g + 1) * STATE].T
    sent = []
    for g in range(GROUPS + 1):
        if g < GROUPS:
            if g % 4 == 0:
                for c in x_in[g : g + 4]:
                    c.wait()
        first = (g - 1) * GROUP_OWNERS
        for w in range(GROUP_COLS // NARROW):
            part = slice(w * NARROW, (w + 1) * NARROW)
            if g < GROUPS:
                weight = spread(scale, g * GROUP_COLS + w * NARROW, NARROW)
                v_buf[g % 2, :, part] = x_buf[g, :, part] * weight.astype(bf16)
            if g > 0:
                s = dot(turned_buf[g - 1], v_buf[(g - 1) % 2, :, part]).astype(bf16)
                below = spread(extra, (g - 1) * GROUP_COLS + w * NARROW, NARROW).astype(bf16)
                for k in range(NARROW // COLS):
                    cols = slice(k * COLS, (k + 1) * COLS)
                    owner = first + w * (NARROW // COLS) + k
                    out_buf[owner, :STATE, :] = s[:, cols]
                    out_buf[owner, STATE:, :] = below[:, cols]
        if g > 0:
            span = pl.ds(first, GROUP_OWNERS)
            sent += copies((out_buf.at[span], out_hbm.at[span], out_sem.at[g - 1]))
    for c in sent:
        c.wait()


def states_of(x, step, decay, inject):
    hbm = pl.BlockSpec(memory_space=pltpu.HBM)
    return pl.pallas_call(
        state_kernel,
        out_shape=jax.ShapeDtypeStruct((OWNERS, ROWS, COLS), bf16),
        in_specs=[hbm] * 4,
        out_specs=hbm,
        scratch_shapes=[
            pltpu.VMEM((GROUPS, TOK, GROUP_COLS), bf16),
            pltpu.VMEM((TOK, HEADS), f32),
            pltpu.VMEM((TOK, HEADS), f32),
            pltpu.VMEM((TOK, GROUPS * STATE), bf16),
            pltpu.VMEM((GROUPS, STATE, TOK), bf16),
            pltpu.VMEM((2, TOK, GROUP_COLS), bf16),
            pltpu.VMEM((OWNERS, ROWS, COLS), bf16),
            pltpu.SemaphoreType.DMA((3,)),
            pltpu.SemaphoreType.DMA((GROUPS,)),
            pltpu.SemaphoreType.DMA((GROUPS,)),
        ],
        compiler_params=pltpu.CompilerParams(vmem_limit_bytes=VMEM_LIMIT),
        cost_estimate=pl.CostEstimate(
            flops=2_000_000_000, bytes_accessed=8_000_000, transcendentals=32768
        ),
        name="states",
    )(x, step, decay, inject)


def decay_row(block):
    return block[STATE : STATE + 1].astype(f32) + block[STATE + 1 : STATE + 2].astype(f32)


def pack_rows(decay):
    row = iota((8, COLS), 0)
    high = decay.astype(bf16).astype(f32)
    return jnp.where(row == 0, high, jnp.where(row == 1, decay - high, 0.0)).astype(bf16)


def total_kernel(in_ref, out_ref):
    state = in_ref[0, :STATE, :].astype(f32)
    decay = decay_row(in_ref[0])
    for i in range(1, OWNERS):
        d = decay_row(in_ref[i])
        state = state * d + in_ref[i, :STATE, :].astype(f32)
        decay = decay * d
    out_ref[:STATE, :] = state.astype(bf16)
    out_ref[STATE:, :] = pack_rows(decay)


def join_kernel(place_ref, own_ref, other_ref, pair_ref):
    second = place_ref[0] % 2 == 1
    own, other = own_ref[...].astype(f32), other_ref[...].astype(f32)
    late = jnp.where(second, own, other)
    early = jnp.where(second, other, own)
    late_decay, early_decay = decay_row(late), decay_row(early)
    pair_ref[:STATE, :] = (late[:STATE] + late_decay * early[:STATE]).astype(bf16)
    pair_ref[STATE:, :] = pack_rows(late_decay * early_decay)


def held_kernel(place_ref, other_ref, pair_ref, in_ref, out_hbm, out_buf, sem):
    place = place_ref[0]
    state = jnp.where(place >= 2, pair_ref[:STATE, :].astype(f32), 0.0)
    other = other_ref[...].astype(f32)
    state = jnp.where(place % 2 == 1, other[:STATE] + decay_row(other) * state, state)
    size = OWNERS // PIECES
    sent = []
    for i in range(OWNERS):
        out_buf[i] = state.astype(bf16)
        if (i + 1) % size == 0:
            span = pl.ds(i + 1 - size, size)
            sent += copies((out_buf.at[span], out_hbm.at[span], sem.at[i // size]))
        if i + 1 < OWNERS:
            state = state * decay_row(in_ref[i]) + in_ref[i, :STATE, :].astype(f32)
    for c in sent:
        c.wait()


def total_of(arrived):
    return pl.pallas_call(
        total_kernel,
        out_shape=jax.ShapeDtypeStruct((ROWS, COLS), bf16),
        compiler_params=pltpu.CompilerParams(vmem_limit_bytes=SMALL_VMEM_LIMIT),
        cost_estimate=pl.CostEstimate(flops=4_000_000, bytes_accessed=2_000_000, transcendentals=0),
        name="total",
    )(arrived)


def pair_of(place, own, other):
    vmem = pl.BlockSpec(memory_space=pltpu.VMEM)
    return pl.pallas_call(
        join_kernel,
        out_shape=jax.ShapeDtypeStruct((ROWS, COLS), bf16),
        in_specs=[pl.BlockSpec(memory_space=pltpu.SMEM), vmem, vmem],
        compiler_params=pltpu.CompilerParams(vmem_limit_bytes=SMALL_VMEM_LIMIT),
        cost_estimate=pl.CostEstimate(flops=100_000, bytes_accessed=100_000, transcendentals=0),
        name="pair",
    )(place, own, other)


def held_of(place, other, pair, arrived):
    vmem = pl.BlockSpec(memory_space=pltpu.VMEM)
    return pl.pallas_call(
        held_kernel,
        out_shape=pltpu.HBM((OWNERS, STATE, COLS), bf16),
        in_specs=[pl.BlockSpec(memory_space=pltpu.SMEM), vmem, vmem, vmem],
        out_specs=pl.BlockSpec(memory_space=pltpu.HBM),
        scratch_shapes=[
            pltpu.VMEM((OWNERS, STATE, COLS), bf16),
            pltpu.SemaphoreType.DMA((PIECES,)),
        ],
        compiler_params=pltpu.CompilerParams(vmem_limit_bytes=HELD_VMEM_LIMIT),
        cost_estimate=pl.CostEstimate(flops=4_000_000, bytes_accessed=4_000_000, transcendentals=0),
        name="held",
    )(place, other, pair, arrived)


def local_kernel(
    part, x_hbm, step_hbm, decay_hbm, inject_hbm, readout_hbm, gain_ref, *rest
):
    if part == 0:
        out_hbm, lead_ref = rest[:2]
    else:
        out_hbm = rest[1]
    x_buf, step_buf, decay_buf, inject_buf, readout_buf, out_buf, sem, in_sem, out_sem = rest[2:]
    decay_in, step_in, inject_in, readout_in = copies(
        (decay_hbm, decay_buf, sem.at[0]),
        (step_hbm, step_buf, sem.at[1]),
        (inject_hbm, inject_buf, sem.at[2]),
        (readout_hbm, readout_buf, sem.at[3]),
    )
    x_in = copies(
        *[
            (
                x_hbm.at[:, pl.ds(part * PART_COLS + n * GROUP_COLS, GROUP_COLS)],
                x_buf.at[n],
                in_sem.at[n],
            )
            for n in range(PART_GROUPS)
        ]
    )
    lower = iota((HALF, HALF), 0) >= iota((HALF, HALF), 1)
    lower_f = jnp.where(lower, 1.0, 0.0).astype(f32)
    decay_in.wait()
    cum_a = sums(lower_f, decay_buf[:HALF])
    cum_b = sums(lower_f, decay_buf[HALF:])
    if part == 0:
        lead_ref[:HALF] = jnp.exp(cum_a)
        lead_ref[HALF:] = jnp.exp(cum_b + cum_a[HALF - 1 : HALF])
    mid = HALF // 2 - 1
    mid_b = cum_b[mid : mid + 1]
    gap_a = cum_a - cum_a[mid : mid + 1]
    gap_b = cum_b - mid_b
    onward = jnp.exp(mid_b + gap_a[HALF - 1 : HALF])
    few = iota((8, HEADS), 0)
    rows = jnp.where(few == 0, onward, gain_ref[...])
    step_in.wait()
    into_a = step_buf[:HALF] * jnp.exp(-gap_a)
    into_b = step_buf[HALF:] * jnp.exp(-gap_b)
    from_a = jnp.exp(gap_a)
    from_b = jnp.exp(gap_b)
    zero = jnp.zeros((HALF, HALF), f32)
    inject_in.wait()
    readout_in.wait()

    def pair(r, i):
        return lax.dot_general(r, i, (((1,), (1,)), ((), ())), preferred_element_type=f32)

    sent = []
    for n in range(PART_GROUPS):
        g = part * PART_GROUPS + n
        state_cols = slice(g * STATE, (g + 1) * STATE)
        inj_a = inject_buf[:HALF, state_cols]
        inj_b = inject_buf[HALF:, state_cols]
        read_a = readout_buf[:HALF, state_cols]
        read_b = readout_buf[HALF:, state_cols]
        near_a = jnp.where(lower, pair(read_a, inj_a), zero).astype(bf16)
        near_b = jnp.concatenate(
            [
                pair(read_b, inj_a).astype(bf16),
                jnp.where(lower, pair(read_b, inj_b), zero).astype(bf16),
            ],
            axis=1,
        )
        x_in[n].wait()
        for k in range(GROUP_COLS // WIDE):
            cols = slice(k * WIDE, (k + 1) * WIDE)
            at = g * GROUP_COLS + k * WIDE
            row = spread(rows, at, WIDE)
            gain = row[1:2]
            x_a = x_buf[n, :HALF, cols].astype(f32)
            x_b = x_buf[n, HALF:, cols].astype(f32)
            v_a = x_a * spread(into_a, at, WIDE)
            v_b = (x_b * spread(into_b, at, WIDE)).astype(bf16)
            res_a = dot(near_a, v_a.astype(bf16))
            res_b = dot(near_b, jnp.concatenate([(v_a * row[0:1]).astype(bf16), v_b], axis=0))
            out_a = res_a * spread(from_a, at, WIDE) + gain * x_a
            out_b = res_b * spread(from_b, at, WIDE) + gain * x_b
            out_buf[n, :HALF, cols] = out_a.astype(bf16)
            out_buf[n, HALF:, cols] = out_b.astype(bf16)
        sent += copies(
            (out_buf.at[n], out_hbm.at[:, pl.ds(g * GROUP_COLS, GROUP_COLS)], out_sem.at[n])
        )
    for c in sent:
        c.wait()


def local_of(part, so_far, x, step, decay, inject, readout, gain):
    hbm = pl.BlockSpec(memory_space=pltpu.HBM)
    vmem = pl.BlockSpec(memory_space=pltpu.VMEM)
    return pl.pallas_call(
        functools.partial(local_kernel, part),
        out_shape=[jax.ShapeDtypeStruct(x.shape, bf16)]
        + ([] if so_far else [jax.ShapeDtypeStruct((TOK, HEADS), f32)]),
        in_specs=[hbm] * 5 + [vmem] + [hbm] * len(so_far),
        input_output_aliases={6: 0} if so_far else {},
        out_specs=[hbm] if so_far else [hbm, vmem],
        scratch_shapes=[
            pltpu.VMEM((PART_GROUPS, TOK, GROUP_COLS), bf16),
            pltpu.VMEM((TOK, HEADS), f32),
            pltpu.VMEM((TOK, HEADS), f32),
            pltpu.VMEM((TOK, GROUPS * STATE), bf16),
            pltpu.VMEM((TOK, GROUPS * STATE), bf16),
            pltpu.VMEM((PART_GROUPS, TOK, GROUP_COLS), bf16),
            pltpu.SemaphoreType.DMA((4,)),
            pltpu.SemaphoreType.DMA((PART_GROUPS,)),
            pltpu.SemaphoreType.DMA((PART_GROUPS,)),
        ],
        compiler_params=pltpu.CompilerParams(vmem_limit_bytes=VMEM_LIMIT),
        cost_estimate=pl.CostEstimate(
            flops=2_000_000_000, bytes_accessed=6_000_000, transcendentals=65536
        ),
        name=f"local{part}",
    )(x, step, decay, inject, readout, gain, *so_far)


def out_kernel(
    lead_ref, readout_ref, held_ref, local_hbm, out_hbm, far_buf, local_buf, out_buf, local_sem, out_sem
):
    local_in = copies(
        *[
            (local_hbm.at[:, pl.ds(g * GROUP_COLS, GROUP_COLS)], local_buf.at[g], local_sem.at[g])
            for g in range(GROUPS)
        ]
    )
    sent = []
    for g in range(GROUPS + 1):
        if g % 2 == 1:
            local_in[g - 1].wait()
            local_in[g].wait()
        if g < GROUPS:
            held = jnp.concatenate(
                [held_ref[g * GROUP_OWNERS + i] for i in range(GROUP_OWNERS)], axis=1
            )
            far_buf[g % 2] = dot(readout_ref[:, g * STATE : (g + 1) * STATE], held).astype(bf16)
        if g > 0:
            for w in range(GROUP_COLS // WIDE):
                part = pl.ds(w * WIDE, WIDE)
                at = (g - 1) * GROUP_COLS + w * WIDE
                lead = spread(lead_ref[...], at, WIDE).astype(bf16)
                far = far_buf[(g - 1) % 2, :, part]
                out_buf[g - 1, :, part] = far * lead + local_buf[g - 1, :, part]
                sent += copies(
                    (
                        out_buf.at[g - 1, :, part],
                        out_hbm.at[:, pl.ds(at, WIDE)],
                        out_sem.at[g - 1, w],
                    )
                )
    for c in sent:
        c.wait()


def outputs_of(lead, readout, held, local):
    hbm = pl.BlockSpec(memory_space=pltpu.HBM)
    vmem = pl.BlockSpec(memory_space=pltpu.VMEM)
    return pl.pallas_call(
        out_kernel,
        out_shape=jax.ShapeDtypeStruct((TOK, HEADS * HEAD_DIM), bf16),
        in_specs=[vmem, vmem, vmem, hbm],
        out_specs=hbm,
        scratch_shapes=[
            pltpu.VMEM((2, TOK, GROUP_COLS), bf16),
            pltpu.VMEM((GROUPS, TOK, GROUP_COLS), bf16),
            pltpu.VMEM((GROUPS, TOK, GROUP_COLS), bf16),
            pltpu.SemaphoreType.DMA((GROUPS,)),
            pltpu.SemaphoreType.DMA((GROUPS, GROUP_COLS // WIDE)),
        ],
        compiler_params=pltpu.CompilerParams(vmem_limit_bytes=OUT_VMEM_LIMIT),
        cost_estimate=pl.CostEstimate(
            flops=2_000_000_000, bytes_accessed=12_000_000, transcendentals=0
        ),
        name="outputs",
    )(lead, readout, held, local)


def swap_runs(v, bits, ways):
    return lax.ppermute(v, "seq", [(i, i ^ (bits * STEP)) for i in range(ways)])


def exchange(v, devices):
    return lax.all_to_all(
        v,
        ("seq", "head"),
        split_axis=0,
        concat_axis=0,
        tiled=True,
        axis_index_groups=[
            list(range(first, first + OWNERS)) for first in range(0, devices, OWNERS)
        ],
    )


def shards(features, step_size, log_decay, inject, readout, skip_gain):
    ways = lax.axis_size("seq")
    devices = ways * lax.axis_size("head")
    args = (features, step_size, log_decay, inject, readout, skip_gain[None, :])
    arrived = exchange(states_of(features, step_size, log_decay, inject), devices)
    local, lead = local_of(0, (), *args)
    arrived, local, lead = lax.optimization_barrier((arrived, local, lead))
    place = (lax.axis_index("seq") // STEP).astype(jnp.int32)[None]
    total = total_of(arrived)
    other = swap_runs(total, 1, ways)
    pair = swap_runs(pair_of(place, total, other), 3, ways)
    held = held_of(place, other, pair, arrived)
    held = exchange(held, devices)
    (local,) = local_of(1, (local,), *args)
    return outputs_of(lead, readout, held, local)


def solution(mesh):
    rows = P(("seq", "head"), None)
    return jax.shard_map(
        shards,
        mesh=mesh,
        in_specs=(rows, rows, rows, rows, rows, P()),
        out_specs=rows,
        check_vma=False,
    )
```
